256 devices in a mesh: gx: 8 (over z_hi, core), gy: 32 (over y, z_lo, x).
Axes of the slice: x: 4, y: 4, z: 8 (z_hi: 4, z_lo: 2; z = z_hi * 2 + z_lo), core: 2. Of those that a mesh axis runs over, the one named last changes fastest.
Arguments:
- density: float32 [256, 16, 4096], P('gx', None, 'gy'), may hold values from 0.5 to 2
- velocity: float32 [3, 256, 16, 4096], P(None, 'gx', None, 'gy'), may hold values from -1.2 to 1.2
- bfield: float32 [3, 256, 16, 4096], P(None, 'gx', None, 'gy'), may hold values from -1.2 to 1.2
- pressure: float32 [256, 16, 4096], P('gx', None, 'gy'), may hold values from 0.5 to 2
- shear_shift: int32 [], replicated, may hold values from 0 to 4095
- remap_weight: int32 [], replicated, may hold values from 0 to 65535
Outputs:
- state: float32 [8, 256, 16, 4096], P(None, 'gx', None, 'gy')
The draws below stay inside these ranges and needn't reach their ends.
All inputs are finite; a program needn't handle non-finite values.
Results may differ from the reference program's by a relative error of at most 0.0003.
Values sent between devices are 32-bit elements; how exact they have to be, the bound alone decides.
A program may use at most 128 MiB of HBM per device.

```python
import math
import jax
import jax.numpy as jnp
from jax import lax

CX = 32
CY = 128
NZ = 16
NX = 256
NY = 4096


def edge_layout():
    row_index = jnp.arange(NX, dtype=jnp.int32) % CX
    column_index = jnp.arange(NY, dtype=jnp.int32) % CY
    row_edge = jnp.logical_or(row_index < 2, row_index >= CX - 2)
    column_edge = jnp.logical_or(column_index < 2, column_index >= CY - 2)
    planted = jnp.logical_or(row_edge[:, None, None], column_edge[None, None, :])
    planted = jnp.broadcast_to(planted, (NX, NZ, NY))
    parity = (jnp.arange(NX, dtype=jnp.int32)[:, None, None] + jnp.arange(NZ, dtype=jnp.int32)[None, :, None] + jnp.arange(NY, dtype=jnp.int32)[None, None, :]) % 2
    parity_sign = 1.0 - 2.0 * parity.astype(jnp.float32)
    return (planted, parity_sign)


def positive_field(key, planted_low, planted_high):
    planted, parity_sign = edge_layout()
    key_flip, key_fill, key_level = jax.random.split(key, 3)
    flip_sign = jnp.where(jax.random.uniform(key_flip, (NX, NZ, NY)) < 0.15, -1.0, 1.0)
    level = planted_low * jnp.exp(jax.random.uniform(key_level, (NX, NZ, NY)) * math.log(planted_high / planted_low))
    extreme = jnp.where(parity_sign * flip_sign > 0.0, planted_high, level)
    filling = 0.5 * jnp.exp(jax.random.uniform(key_fill, (NX, NZ, NY)) * math.log(4.0))
    return jnp.where(planted, extreme, filling).astype(jnp.float32)


def vector_field(key):
    planted, parity_sign = edge_layout()
    key_flip, key_comp, key_fill = jax.random.split(key, 3)
    flip_sign = jnp.where(jax.random.uniform(key_flip, (3, NX, NZ, NY)) < 0.15, -1.0, 1.0)
    component_sign = jnp.where(jax.random.uniform(key_comp, (3, 1, 1, 1)) < 0.5, -1.0, 1.0)
    extreme = 1.2 * component_sign * flip_sign * parity_sign[None]
    filling = jnp.clip(0.3 * jax.random.normal(key_fill, (3, NX, NZ, NY)), -1.2, 1.2)
    return jnp.where(planted[None], extreme, filling).astype(jnp.float32)


def draw_density(key, part):
    return positive_field(jax.random.fold_in(key, 37), 0.5, 2.0)


def draw_pressure(key, part):
    return positive_field(jax.random.fold_in(key, 41), 1.2, 2.0)


def draw_velocity(key, part):
    return vector_field(jax.random.fold_in(key, 11))


def draw_bfield(key, part):
    return vector_field(jax.random.fold_in(key, 23))


def setup_inputs(seed: int = 0) -> dict:
    splits = jax.random.split(jax.random.key(seed), 7)
    density = draw_density(jax.random.fold_in(splits[6], 71), 0)
    velocity = draw_velocity(jax.random.fold_in(splits[6], 71), 0)
    bfield = draw_bfield(jax.random.fold_in(splits[6], 71), 0)
    pressure = draw_pressure(jax.random.fold_in(splits[6], 71), 0)
    shear_shift = jax.random.randint(splits[4], (), 0, NY).astype(jnp.int32)
    remap_weight = jax.random.randint(splits[5], (), 0, 65536).astype(jnp.int32)
    return {"density": density, "velocity": velocity, "bfield": bfield, "pressure": pressure, "shear_shift": shear_shift, "remap_weight": remap_weight}


GAMMA = 5.0 / 3.0
SHEAR_Q = 1.5
TIME_STEP = 0.03
WEIGHT_SCALE = 1.0 / 65536.0

def minmod(upper, lower):
    return jnp.where(upper * lower > 0.0, jnp.sign(upper) * jnp.minimum(jnp.abs(upper), jnp.abs(lower)), 0.0)

def to_primitive(conserved):
    density = conserved[0]
    velocity = conserved[1:4] / density
    magnetic = conserved[4:7]
    pressure = (GAMMA - 1.0) * (conserved[7] - 0.5 * density * lax.optimization_barrier(jnp.sum(velocity * velocity, axis=0)) - 0.5 * lax.optimization_barrier(jnp.sum(magnetic * magnetic, axis=0)))
    return jnp.concatenate([density[None], velocity, magnetic, pressure[None]], axis=0)

def point_flux(primitive, normal_axis):
    density = primitive[0]
    velocity = primitive[1:4]
    magnetic = primitive[4:7]
    pressure = primitive[7]
    mag_square = lax.optimization_barrier(jnp.sum(magnetic * magnetic, axis=0))
    total_pressure = pressure + 0.5 * mag_square
    energy = pressure / (GAMMA - 1.0) + 0.5 * density * lax.optimization_barrier(jnp.sum(velocity * velocity, axis=0)) + 0.5 * mag_square
    normal_speed = velocity[normal_axis]
    normal_field = magnetic[normal_axis]
    velocity_dot = lax.optimization_barrier(jnp.sum(velocity * magnetic, axis=0))
    momentum_flux = []
    induction_flux = []
    for component in range(3):
        term = density * velocity[component] * normal_speed - normal_field * magnetic[component]
        if component == normal_axis:
            term = term + total_pressure
        momentum_flux.append(term)
        induction_flux.append(normal_speed * magnetic[component] - normal_field * velocity[component])
    energy_flux = (energy + total_pressure) * normal_speed - normal_field * velocity_dot
    flux = jnp.stack([density * normal_speed] + momentum_flux + induction_flux + [energy_flux])
    conserved = jnp.stack([density, density * velocity[0], density * velocity[1], density * velocity[2], magnetic[0], magnetic[1], magnetic[2], energy])
    sound_square = GAMMA * pressure / density
    alfven_square = mag_square / density
    transverse = jnp.zeros_like(density)
    for component in range(3):
        if component != normal_axis:
            transverse = transverse + magnetic[component] * magnetic[component]
    transverse = transverse / density
    spread = sound_square - alfven_square
    fast_speed = jnp.sqrt(0.5 * (sound_square + alfven_square + jnp.sqrt(spread * spread + 4.0 * sound_square * transverse)))
    return (flux, conserved, jnp.abs(normal_speed) + fast_speed)

def slab(array, start, stop, axis):
    return lax.slice_in_dim(array, start, stop, axis=axis)

def flux_difference(primitive, axis, normal_axis):
    length = primitive.shape[axis] - 4
    upper = slab(primitive, 2, length + 4, axis) - slab(primitive, 1, length + 3, axis)
    lower = slab(primitive, 1, length + 3, axis) - slab(primitive, 0, length + 2, axis)
    slopes = minmod(upper, lower)
    left_state = slab(primitive, 1, length + 2, axis) + 0.5 * slab(slopes, 0, length + 1, axis)
    right_state = slab(primitive, 2, length + 3, axis) - 0.5 * slab(slopes, 1, length + 2, axis)
    flux_left, cons_left, speed_left = point_flux(left_state, normal_axis)
    flux_right, cons_right, speed_right = point_flux(right_state, normal_axis)
    speed = jnp.maximum(speed_left, speed_right)
    face = 0.5 * (flux_left + flux_right) - 0.5 * speed * (cons_right - cons_left)
    return slab(face, 1, length + 1, axis) - slab(face, 0, length, axis)

def source_terms(conserved, radial, omega):
    zeros = jnp.zeros_like(conserved[0])
    momentum_x = 2.0 * omega * conserved[2] + 2.0 * SHEAR_Q * omega * omega * conserved[0] * radial
    momentum_y = -2.0 * omega * conserved[1]
    energy = 2.0 * SHEAR_Q * omega * omega * radial * conserved[1]
    return jnp.stack([zeros, momentum_x, momentum_y, zeros, zeros, zeros, zeros, energy])

def boost(conserved, delta):
    momentum_y = conserved[2] + conserved[0] * delta
    energy = conserved[7] + conserved[2] * delta + 0.5 * conserved[0] * delta * delta
    return jnp.stack([conserved[0], conserved[1], momentum_y, conserved[3], conserved[4], conserved[5], conserved[6], energy])

def remap(source, shift, weight):
    return (1.0 - weight) * jnp.roll(source, shift, axis=3) + weight * jnp.roll(source, shift + 1, axis=3)

def pad_periodic(array, axis):
    total = array.shape[axis]
    return jnp.concatenate([slab(array, total - 2, total, axis), array, slab(array, 0, 2, axis)], axis=axis)

def section_rate(conserved, shift, weight, omega, radial):
    other_shift = (NY - 1 - shift).astype(jnp.int32)
    other_weight = 1.0 - weight
    left = boost(remap(conserved[:, NX - 2:], shift, weight), 1.0)
    right = boost(remap(conserved[:, :2], other_shift, other_weight), -1.0)
    radial_pad = jnp.concatenate([left, conserved, right], axis=1)
    change = flux_difference(to_primitive(pad_periodic(conserved, 3)), 3, 1)
    change = change + flux_difference(to_primitive(pad_periodic(conserved, 2)), 2, 2)
    change = change + flux_difference(to_primitive(radial_pad), 1, 0)
    return source_terms(conserved, radial, omega) - change

def reference(density, velocity, bfield, pressure, shear_shift, remap_weight):
    omega = 1.0 / (SHEAR_Q * NX)
    radial = (jnp.arange(NX).astype(jnp.float32) + 0.5 - 0.5 * NX)[:, None, None]
    weight = remap_weight.astype(jnp.float32) * WEIGHT_SCALE
    shift = shear_shift.astype(jnp.int32)
    speed_y = velocity[1] - SHEAR_Q * omega * radial
    moving = jnp.stack([velocity[0], speed_y, velocity[2]])
    energy = pressure / (GAMMA - 1.0) + 0.5 * density * lax.optimization_barrier(jnp.sum(moving * moving, axis=0)) + 0.5 * lax.optimization_barrier(jnp.sum(bfield * bfield, axis=0))
    start_state = jnp.concatenate([density[None], density[None] * moving, bfield, energy[None]], axis=0)
    middle = start_state + TIME_STEP * section_rate(start_state, shift, weight, omega, radial)
    final = 0.5 * start_state + 0.5 * (middle + TIME_STEP * section_rate(middle, shift, weight, omega, radial))
    return final
```

```python
import functools

import jax
import jax.numpy as jnp
from jax import lax
from jax.experimental import pallas as pl
from jax.experimental.pallas import tpu as pltpu
from jax.sharding import PartitionSpec as P

GAMMA = 5.0 / 3.0
SHEAR_Q = 1.5
TIME_STEP = 0.03
WEIGHT_SCALE = 1.0 / 65536.0
TINY = 1e-30
MESH = pl.DeviceIdType.MESH
DIGITS = {32: ((4, 1), (2, 4), (4, 8)), 8: ((2, 1), (2, 2), (2, 4))}
CUTS = (2, 12, 19, 28)


def limited(upper, lower):
    return jnp.minimum(jnp.maximum(upper, jnp.minimum(lower, 0.0)), jnp.maximum(lower, 0.0))


def side_flux(state, n):
    rho, v, b, p = state[0], state[1:4], state[4:7], state[7]
    a, c = [t for t in range(3) if t != n]
    m = [rho * v[t] for t in range(3)]
    vn, bn = v[n], b[n]
    bn2 = bn * bn
    bt2 = b[a] * b[a] + b[c] * b[c]
    b2 = bt2 + bn2
    hb2 = 0.5 * b2
    pg = p + 0.5 * (p + (m[0] * v[0] + m[1] * v[1] + m[2] * v[2]))
    energy = pg + hb2
    fba = vn * b[a] - bn * v[a]
    fbc = vn * b[c] - bn * v[c]
    flux = [None] * 8
    flux[0] = m[n]
    flux[1 + n] = m[n] * vn - bn2 + (p + hb2)
    flux[1 + a] = m[n] * v[a] - bn * b[a]
    flux[1 + c] = m[n] * v[c] - bn * b[c]
    flux[4 + a] = fba
    flux[4 + c] = fbc
    flux[7] = (pg + p) * vn + (b[a] * fba + b[c] * fbc)
    gp = GAMMA * p
    total = gp + b2
    spread = gp - b2
    inner = spread * spread + (4.0 * GAMMA * p) * bt2
    twice = total + inner * lax.rsqrt(jnp.maximum(inner, TINY))
    fast = twice * lax.rsqrt(jnp.maximum((rho + rho) * twice, TINY))
    return flux, [rho, *m, *b, energy], jnp.abs(vn) + fast


def face_flux(left, right, n):
    fl, ul, sl = side_flux(left, n)
    fr, ur, sr = side_flux(right, n)
    speed = jnp.maximum(sl, sr)
    out = []
    for k in range(8):
        jump = speed * (ur[k] - ul[k])
        out.append(-jump if fl[k] is None else (fl[k] + fr[k]) - jump)
    return out


def to_primitive(u):
    inv = 1.0 / u[0]
    v = [u[k] * inv for k in (1, 2, 3)]
    kin = u[1] * v[0] + u[2] * v[1] + u[3] * v[2]
    mag = u[4] * u[4] + u[5] * u[5] + u[6] * u[6]
    return [u[0], *v, u[4], u[5], u[6], (GAMMA - 1.0) * (u[7] - 0.5 * (kin + mag))]


def kernel(
    nx, ny, shift_ref, weight_ref, rho_ref, vel_ref, mag_ref, pre_ref, out_ref,
    u0, u1, w, wh, sd, sl, sf, pack, patch, xg, yg, st00, st01, st02, st10, st11, st12, ts, tb,
    xs, xr, ys, yr, cs, cr, tsem, trec,
):
    rows, nz, wide = rho_ref.shape
    half = nz // 2
    total_x = nx * rows
    total_y = ny * wide
    omega = 1.0 / (SHEAR_Q * total_x)
    digits = DIGITS[ny]
    stages = ((st00, st01, st02), (st10, st11, st12))
    gx = lax.axis_index("gx")
    gy = lax.axis_index("gy")
    first = gx == 0
    last = gx == nx - 1
    edge = jnp.logical_or(first, last)
    other = jnp.where(first, nx - 1, 0)
    north = lax.rem(gy + 1, ny)
    south = lax.rem(gy + ny - 1, ny)
    mine = [lax.rem(lax.div(gy, stride), radix) for radix, stride in digits]
    lane = lax.broadcasted_iota(jnp.int32, (2, half, wide), 2)
    quad = jnp.bitwise_and(lane, 3)
    group = lax.shift_right_logical(lane, 2)
    inside = jnp.logical_and(lane >= 2, lane < wide - 2)

    def digit_peer(stage, step):
        radix, stride = digits[stage]
        digit = lax.rem(mine[stage] + step, radix)
        return digit, gy + (digit - mine[stage]) * stride

    barrier = pltpu.get_barrier_semaphore()

    def greet(x, y):
        pl.semaphore_signal(barrier, inc=1, device_id=(x, y), device_id_type=MESH)

    greet(gx, north)
    greet(gx, south)

    @pl.when(gx > 0)
    def _():
        greet(gx - 1, gy)

    @pl.when(gx < nx - 1)
    def _():
        greet(gx + 1, gy)

    far = 3 + sum(radix - 1 for radix, _ in digits)

    @pl.when(edge)
    def _():
        for stage in range(3):
            for step in range(1, digits[stage][0]):
                greet(gx, digit_peer(stage, step)[1])
        for y in (south, gy, north):
            greet(other, y)

    def await_greetings():
        pl.semaphore_wait(barrier, jnp.where(edge, 3 + far, 4))

    def remote(src, dst, send, recv, x, y):
        return pltpu.make_async_remote_copy(
            src_ref=src, dst_ref=dst, send_sem=send, recv_sem=recv, device_id=(x, y), device_id_type=MESH
        )

    def radial(i):
        return (gx * rows + i).astype(jnp.float32) + (0.5 - 0.5 * total_x)

    def put_primitive(i, prim):
        for k in range(8):
            w[k, i + 2] = prim[k]
            wh[k, i + 2] = 0.5 * prim[k]

    def collect(i, prim, packs):
        turn = jnp.bitwise_and(4 * i + 4, wide - 1)
        here = group == i
        after = group == jnp.bitwise_and(i + 1, wide // 4 - 1)
        moved = [pltpu.roll(prim[k], turn, 2) for k in range(8)]
        left = [jnp.where(after, moved[k], packs[k]) for k in range(8)]
        right = [jnp.where(here, moved[k], packs[8 + k]) for k in range(8)]
        return (*left, *right)

    def store_packs(sec, packs):
        for k in range(8):
            pack[sec, 0, k] = pltpu.roll(packs[k], wide - 4, 2)
            pack[sec, 1, k] = packs[8 + k]

    def start_row(i, packs):
        def load(ref, *lead):
            return jnp.stack([ref[(*lead, i, pl.ds(z, half, stride=2), slice(None))] for z in range(2)])

        rho = load(rho_ref)
        v = [load(vel_ref, 0), load(vel_ref, 1) - SHEAR_Q * omega * radial(i), load(vel_ref, 2)]
        b = [load(mag_ref, k) for k in range(3)]
        p = load(pre_ref)
        m = [rho * v[k] for k in range(3)]
        kin = m[0] * v[0] + m[1] * v[1] + m[2] * v[2]
        mag = b[0] * b[0] + b[1] * b[1] + b[2] * b[2]
        energy = p * (1.0 / (GAMMA - 1.0)) + 0.5 * (kin + mag)
        for k, value in enumerate([rho, *m, *b, energy]):
            u0[k, i] = value
        prim = [rho, *v, *b, p]
        put_primitive(i, prim)
        return collect(i, prim, packs)

    def merged(i, ref, k):
        back = pltpu.roll(patch[k], jnp.bitwise_and(wide - 2 - 4 * i, wide - 1), 2)
        return ref[k, i] + jnp.where(inside, 0.0, back)

    def middle_row(i, packs):
        u = [merged(i, u1, k) for k in range(8)]
        for k in range(8):
            u1[k, i] = u[k]
        prim = to_primitive(u)
        put_primitive(i, prim)
        return collect(i, prim, packs)

    def final_row(i, carry):
        for k in range(8):
            value = merged(i, u0, k)
            for z in range(2):
                out_ref[k, i, pl.ds(z, half, stride=2), :] = value[z]
        return carry

    def z_up(x):
        return jnp.stack([x[1], pltpu.roll(x[0], half - 1, 0)])

    def z_down(x):
        return jnp.stack([pltpu.roll(x[1], 1, 0), x[0]])

    def y_up(x):
        return pltpu.roll(x, wide - 1, 2)

    def y_down(x):
        return pltpu.roll(x, 1, 2)

    def periodic(whole, halved, n, up, down):
        left, right = [], []
        for k in range(8):
            d = up(halved[k]) - halved[k]
            h = limited(d, down(d))
            left.append(whole[k] + h)
            right.append(up(whole[k] - h))
        face = face_flux(left, right, n)
        return [f - down(f) for f in face]

    def x_face(i):
        left, right = [], []
        for k in range(8):
            d = wh[k, i + 4] - wh[k, i + 3]
            h = limited(d, sd[k])
            here = w[k, i + 3]
            left.append(sl[k])
            right.append(here - h)
            sd[k] = d
            sl[k] = here + h
        return face_flux(left, right, 0)

    def x_begin(i):
        for k in range(8):
            before = wh[k, i + 1] - wh[k, i]
            d = wh[k, i + 2] - wh[k, i + 1]
            sd[k] = d
            sl[k] = w[k, i + 1] + limited(d, before)
        face = x_face(i - 1)
        for k in range(8):
            sf[k] = face[k]

    def main_row(sec, i, carry):
        whole = [w[k, i + 2] for k in range(8)]
        halved = [wh[k, i + 2] for k in range(8)]
        dz = periodic(whole, halved, 2, z_up, z_down)
        dy = periodic(whole, halved, 1, y_up, y_down)
        fx = x_face(i)
        change = []
        for k in range(8):
            change.append((dz[k] + jnp.where(inside, dy[k], 0.0)) + (fx[k] - sf[k]))
            sf[k] = fx[k]
        ref = u1 if sec else u0
        u = [ref[k, i] for k in range(8)]
        step = 0.5 * TIME_STEP if sec else TIME_STEP
        r = radial(i)
        pull = (2.0 * SHEAR_Q * omega * omega * step) * r
        source = {
            1: (2.0 * omega * step) * u[2] + pull * u[0],
            2: (-2.0 * omega * step) * u[1],
            7: pull * u[1],
        }
        for k in range(8):
            base = 0.5 * (u0[k, i] + u[k]) if sec else u[k]
            value = base - (0.5 * step) * change[k]
            if k in source:
                value = value + source[k]
            (u0 if sec else u1)[k, i] = value
        return carry

    def edge_patch(sec):
        step = 0.5 * TIME_STEP if sec else TIME_STEP

        def turned(x, by):
            return x if by % wide == 0 else pltpu.roll(x, by % wide, 2)

        def rates(low, high, base):
            left, right = [], []
            for k in range(8):
                col = []
                for t in range(-1, 3):
                    start = t - base
                    take = quad < -start
                    if start >= 0:
                        col.append(turned(high[k], -start))
                    elif start == -4:
                        col.append(low[k])
                    elif start < -4:
                        col.append(turned(low[k], -4 - start))
                    else:
                        col.append(jnp.where(take, turned(low[k], -4 - start), turned(high[k], -start)))
                d = [0.5 * (col[t + 1] - col[t]) for t in range(3)]
                left.append(col[1] + limited(d[1], d[0]))
                right.append(col[2] - limited(d[2], d[1]))
            face = face_flux(left, right, 1)
            return [f - pltpu.roll(f, 1, 2) for f in face]

        low_side = rates([yg[sec, 0, k] for k in range(8)], [pack[sec, 0, k] for k in range(8)], 2)
        high_side = rates([pack[sec, 1, k] for k in range(8)], [yg[sec, 1, k] for k in range(8)], 4)
        for k in range(8):
            both = jnp.where(quad < 2, pltpu.roll(high_side[k], wide - 2, 2), low_side[k])
            patch[k] = (-0.5 * step) * both

    shift = shift_ref[0]
    weight = weight_ref[0].astype(jnp.float32) * WEIGHT_SCALE
    out_shift = jnp.where(first, total_y - 1 - shift, shift)
    in_shift = jnp.where(first, shift, total_y - 1 - shift)
    in_weight = jnp.where(first, weight, 1.0 - weight)
    blocks = lax.div(out_shift, wide)
    picks = []
    for d, (radix, _) in enumerate(digits):
        part = lax.rem(blocks, radix)
        picks.append(lax.rem(mine[d] - part + radix, radix))
        blocks = lax.div(blocks, radix) + (mine[d] < part).astype(jnp.int32)

    def stage_copies(sec, stage, incoming):
        ref = stages[sec][stage]
        copies = []
        for step in range(1, digits[stage][0]):
            digit, y = digit_peer(stage, step)
            slot = digit if incoming else mine[stage]
            copies.append(
                remote(
                    ref.at[mine[stage]], ref.at[slot],
                    cs.at[sec, stage, step - 1], cr.at[sec, stage, slot], gx, y,
                )
            )
        return copies

    def transit_copies(sec):
        return [
            remote(ts.at[sec], tb.at[sec, 0], tsem.at[sec, 0], trec.at[sec, 0], other, gy),
            remote(ts.at[sec], tb.at[sec, 1], tsem.at[sec, 1], trec.at[sec, 1], other, north),
        ]

    def chain_start(sec, u):
        @pl.when(first)
        def _():
            for k in range(8):
                stages[sec][0][mine[0], k] = u[k, 0:2]

        @pl.when(last)
        def _():
            for k in range(8):
                stages[sec][0][mine[0], k] = u[k, rows - 2 : rows]

        @pl.when(edge)
        def _():
            for copy in stage_copies(sec, 0, False):
                copy.start()

    def chain_step(sec, stage):
        @pl.when(edge)
        def _():
            for copy in stage_copies(sec, stage, True):
                copy.wait_recv()
            for k in range(8):
                value = stages[sec][stage][picks[stage], k]
                if stage < 2:
                    stages[sec][stage + 1][mine[stage + 1], k] = value
                else:
                    ts[sec, k] = value
            for copy in stage_copies(sec, stage + 1, False) if stage < 2 else transit_copies(sec):
                copy.start()

    def chain_end(sec):
        @pl.when(edge)
        def _():
            for copy in transit_copies(sec):
                copy.wait_recv()
            inner = lax.rem(in_shift, wide)
            src = lax.broadcasted_iota(jnp.int32, (wide, wide), 0)
            dst = lax.broadcasted_iota(jnp.int32, (wide, wide), 1)
            gap = dst - src - inner
            near = jnp.where(gap == 0, 1.0 - in_weight, 0.0) + jnp.where(gap == 1, in_weight, 0.0)
            back = jnp.where(gap == -wide, 1.0 - in_weight, 0.0) + jnp.where(gap == 1 - wide, in_weight, 0.0)
            flat = (8 * 2 * 2 * half, wide)

            def times(x, m):
                return jnp.dot(x, m, precision=lax.Precision.HIGHEST, preferred_element_type=jnp.float32)

            ghost = times(tb[sec, 0].reshape(flat), near) + times(tb[sec, 1].reshape(flat), back)
            ghost = ghost.reshape(8, 2, 2, half, wide)
            delta = jnp.where(first, 1.0, -1.0)
            start = jnp.where(first, 0, rows + 2)
            for j in range(2):
                u = [ghost[k, j] for k in range(8)]
                momentum = u[2] + u[0] * delta
                u[7] = u[7] + u[2] * delta + 0.5 * u[0]
                u[2] = momentum
                put_primitive(start + j - 2, to_primitive(u))

    def x_copy(sec, side, incoming):
        away = gx - 1 if side == 0 else gx + 1
        own = w.at[:, 2:4] if side == 0 else w.at[:, rows : rows + 2]
        slot = side if incoming else 1 - side
        return remote(own, xg.at[sec, slot], xs.at[sec, side], xr.at[sec, slot], away, gy)

    def y_copy(sec, side, incoming):
        away = south if side == 0 else north
        slot = side if incoming else 1 - side
        return remote(pack.at[sec, side], yg.at[sec, slot], ys.at[sec, side], yr.at[sec, slot], gx, away)

    def on_side(side, do):
        pl.when(gx > 0 if side == 0 else gx < nx - 1)(do)

    def outer_row(t):
        return jnp.where(t < 2, t, t + rows - 4)

    empty = tuple(jnp.zeros((2, half, wide), jnp.float32) for _ in range(16))

    for sec in range(2):
        one_row = middle_row if sec else start_row
        packs = lax.fori_loop(0, 4, lambda t, c: one_row(outer_row(t), c), empty)
        if sec == 0:
            await_greetings()
        chain_start(sec, u1 if sec else u0)
        for side in range(2):
            on_side(side, lambda: x_copy(sec, side, False).start())
        packs = lax.fori_loop(2, rows - 2, one_row, packs)
        store_packs(sec, packs)
        x_begin(2)
        for side in range(2):
            y_copy(sec, side, False).start()
        row = functools.partial(main_row, sec)
        cuts = [min(c * rows // 32, rows - 2) for c in CUTS] + [rows - 2]
        cuts[0] = 2
        for stage in range(3):
            lax.fori_loop(cuts[stage], cuts[stage + 1], row, 0)
            chain_step(sec, stage)
        lax.fori_loop(cuts[3], cuts[4], row, 0)
        for side in range(2):
            y_copy(sec, side, True).wait_recv()
        edge_patch(sec)
        for side in range(2):

            def take():
                x_copy(sec, side, True).wait_recv()
                for k in range(8):
                    value = xg[sec, side, k]
                    start = 0 if side == 0 else rows + 2
                    w[k, start : start + 2] = value
                    wh[k, start : start + 2] = 0.5 * value

            on_side(side, take)
        chain_end(sec)
        lax.fori_loop(rows - 2, rows, row, 0)
        x_begin(0)
        lax.fori_loop(0, 2, row, 0)
        for side in range(2):
            on_side(side, lambda: x_copy(sec, side, False).wait_send())
            y_copy(sec, side, False).wait_send()
    lax.fori_loop(0, rows, final_row, 0)

    @pl.when(edge)
    def _():
        for sec in range(2):
            for stage in range(3):
                for copy in stage_copies(sec, stage, False):
                    copy.wait_send()
            for copy in transit_copies(sec):
                copy.wait_send()


def solution(mesh):
    nx, ny = mesh.shape["gx"], mesh.shape["gy"]

    def on_device(density, velocity, bfield, pressure, shear_shift, remap_weight):
        rows, nz, wide = density.shape
        half = nz // 2
        tile = (2, half, wide)
        radices = [radix for radix, _ in DIGITS[ny]]
        slab = (8, 2, *tile)
        f32 = jnp.float32
        dma = pltpu.SemaphoreType.DMA
        vmem = pl.BlockSpec(memory_space=pltpu.VMEM)
        smem = pl.BlockSpec(memory_space=pltpu.SMEM)
        return pl.pallas_call(
            functools.partial(kernel, nx, ny),
            out_shape=jax.ShapeDtypeStruct((8, rows, nz, wide), f32),
            in_specs=[smem, smem, vmem, vmem, vmem, vmem],
            out_specs=vmem,
            scratch_shapes=[
                pltpu.VMEM((8, rows, *tile), f32),
                pltpu.VMEM((8, rows, *tile), f32),
                pltpu.VMEM((8, rows + 4, *tile), f32),
                pltpu.VMEM((8, rows + 4, *tile), f32),
                pltpu.VMEM((8, *tile), f32),
                pltpu.VMEM((8, *tile), f32),
                pltpu.VMEM((8, *tile), f32),
                pltpu.VMEM((2, 2, 8, *tile), f32),
                pltpu.VMEM((8, *tile), f32),
                pltpu.VMEM((2, 2, *slab), f32),
                pltpu.VMEM((2, 2, 8, *tile), f32),
                *[pltpu.VMEM((radix, *slab), f32) for radix in radices * 2],
                pltpu.VMEM((2, *slab), f32),
                pltpu.VMEM((2, 2, *slab), f32),
                dma((2, 2)),
                dma((2, 2)),
                dma((2, 2)),
                dma((2, 2)),
                dma((2, 3, 3)),
                dma((2, 3, 4)),
                dma((2, 2)),
                dma((2, 2)),
            ],
            compiler_params=pltpu.CompilerParams(
                collective_id=0, has_side_effects=True, vmem_limit_bytes=60 * 1024 * 1024
            ),
        )(shear_shift.reshape(1), remap_weight.reshape(1), density, velocity, bfield, pressure)

    placed = (
        P("gx", None, "gy"),
        P(None, "gx", None, "gy"),
        P(None, "gx", None, "gy"),
        P("gx", None, "gy"),
        P(),
        P(),
    )
    return jax.shard_map(
        on_device, mesh=mesh, in_specs=placed, out_specs=P(None, "gx", None, "gy"), check_vma=False
    )
```

```python
import functools

import jax
import jax.numpy as jnp
from jax import lax
from jax.experimental import pallas as pl
from jax.experimental.pallas import tpu as pltpu
from jax.sharding import PartitionSpec as P

GAMMA = 5.0 / 3.0
SHEAR_Q = 1.5
TIME_STEP = 0.03
WEIGHT_SCALE = 1.0 / 65536.0
TINY = 1e-30
MESH = pl.DeviceIdType.MESH
CUT = 12


def limited(upper, lower):
    return jnp.minimum(jnp.maximum(upper, jnp.minimum(lower, 0.0)), jnp.maximum(lower, 0.0))


def side_flux(state, n):
    rho, v, b, p = state[0], state[1:4], state[4:7], state[7]
    a, c = [t for t in range(3) if t != n]
    m = [rho * v[t] for t in range(3)]
    vn, bn = v[n], b[n]
    bn2 = bn * bn
    bt2 = b[a] * b[a] + b[c] * b[c]
    b2 = bt2 + bn2
    hb2 = 0.5 * b2
    pg = p + 0.5 * (p + (m[0] * v[0] + m[1] * v[1] + m[2] * v[2]))
    energy = pg + hb2
    fba = vn * b[a] - bn * v[a]
    fbc = vn * b[c] - bn * v[c]
    flux = [None] * 8
    flux[0] = m[n]
    flux[1 + n] = m[n] * vn - bn2 + (p + hb2)
    flux[1 + a] = m[n] * v[a] - bn * b[a]
    flux[1 + c] = m[n] * v[c] - bn * b[c]
    flux[4 + a] = fba
    flux[4 + c] = fbc
    flux[7] = (pg + p) * vn + (b[a] * fba + b[c] * fbc)
    gp = GAMMA * p
    total = gp + b2
    spread = gp - b2
    inner = spread * spread + (4.0 * GAMMA * p) * bt2
    twice = total + inner * lax.rsqrt(jnp.maximum(inner, TINY))
    fast = twice * lax.rsqrt(jnp.maximum((rho + rho) * twice, TINY))
    return flux, [rho, *m, *b, energy], jnp.abs(vn) + fast


def face_flux(left, right, n):
    fl, ul, sl = side_flux(left, n)
    fr, ur, sr = side_flux(right, n)
    speed = jnp.maximum(sl, sr)
    out = []
    for k in range(8):
        jump = speed * (ur[k] - ul[k])
        out.append(-jump if fl[k] is None else (fl[k] + fr[k]) - jump)
    return out


def to_primitive(u):
    inv = 1.0 / u[0]
    v = [u[k] * inv for k in (1, 2, 3)]
    kin = u[1] * v[0] + u[2] * v[1] + u[3] * v[2]
    mag = u[4] * u[4] + u[5] * u[5] + u[6] * u[6]
    return [u[0], *v, u[4], u[5], u[6], (GAMMA - 1.0) * (u[7] - 0.5 * (kin + mag))]


def kernel(
    nx, ny, shift_ref, weight_ref, rho_in, vel_in, mag_in, pre_in, out_ref, rho_ref, vel_ref, mag_ref, pre_ref,
    u0, u1, w, wh, sd, sl, sf, pack, patch, xg, yg, out0, ring0, back0, got0, out1, ring1, back1, got1,
    xs, xr, ys, yr, ss, sr, ls,
):
    rows, nz, wide = rho_ref.shape
    half = nz // 2
    total_x = nx * rows
    total_y = ny * wide
    omega = 1.0 / (SHEAR_Q * total_x)
    share = 32 // ny
    spread = ((out0, ring0, back0, got0), (out1, ring1, back1, got1))
    gx = lax.axis_index("gx")
    gy = lax.axis_index("gy")
    first = gx == 0
    last = gx == nx - 1
    edge = jnp.logical_or(first, last)
    other = jnp.where(first, nx - 1, 0)
    north = lax.rem(gy + 1, ny)
    south = lax.rem(gy + ny - 1, ny)
    lane = lax.broadcasted_iota(jnp.int32, (2, half, wide), 2)
    quad = jnp.bitwise_and(lane, 3)
    even = jnp.bitwise_and(lane, 4) == 0
    inside = jnp.logical_and(lane >= 2, lane < wide - 2)

    loads = [
        pltpu.make_async_copy(src, dst, ls.at[k])
        for k, (src, dst) in enumerate(
            [(rho_in, rho_ref), (vel_in, vel_ref), (mag_in, mag_ref), (pre_in, pre_ref)]
        )
    ]
    for load in loads:
        load.start()

    barrier = pltpu.get_barrier_semaphore()

    def greet(x, y):
        pl.semaphore_signal(barrier, inc=1, device_id=(x, y), device_id_type=MESH)

    greet(gx, north)
    greet(gx, south)

    @pl.when(gx > 0)
    def _():
        greet(gx - 1, gy)

    @pl.when(gx < nx - 1)
    def _():
        greet(gx + 1, gy)

    def each(low, high, do):
        def body(t, carry):
            do(t)
            return carry

        lax.fori_loop(low, high, body, 0)

    def peer(step):
        return lax.rem(gy + step, ny)

    @pl.when(edge)
    def _():
        each(1, ny, lambda step: greet(gx, peer(step)))
        each(0, ny, lambda step: greet(other, peer(step)))

    def await_greetings():
        pl.semaphore_wait(barrier, jnp.where(edge, 2 + 2 * ny, 4))

    def remote(src, dst, send, recv, x, y):
        return pltpu.make_async_remote_copy(
            src_ref=src, dst_ref=dst, send_sem=send, recv_sem=recv, device_id=(x, y), device_id_type=MESH
        )

    def radial(i):
        return (gx * rows + i).astype(jnp.float32) + (0.5 - 0.5 * total_x)

    def put_primitive(i, prim):
        for k in range(8):
            w[k, i + 2] = prim[k]
            wh[k, i + 2] = 0.5 * prim[k]

    def store_packs(sec):
        def some(t, carry):
            for k in (2 * t, 2 * t + 1):
                both = []
                for odd in range(2):
                    acc = jnp.zeros((2, half, wide), jnp.float32)
                    slot = lax.shift_right_logical(jnp.bitwise_and(lane - 4 * odd, wide - 1), 3)
                    for i in range(odd, rows, 2):
                        moved = pltpu.roll(w[k, i + 2], (4 * i + 4) % wide, 2)
                        acc = jnp.where(slot == i // 2, moved, acc)
                    both.append(acc)
                pack[sec, 0, k] = pltpu.roll(jnp.where(even, both[1], both[0]), wide - 4, 2)
                pack[sec, 1, k] = jnp.where(even, both[0], both[1])
            return carry

        lax.fori_loop(0, 4, some, 0)

    def start_row(i):
        def load(ref, *lead):
            return jnp.stack([ref[(*lead, i, pl.ds(z, half, stride=2), slice(None))] for z in range(2)])

        rho = load(rho_ref)
        v = [load(vel_ref, 0), load(vel_ref, 1) - SHEAR_Q * omega * radial(i), load(vel_ref, 2)]
        b = [load(mag_ref, k) for k in range(3)]
        p = load(pre_ref)
        m = [rho * v[k] for k in range(3)]
        kin = m[0] * v[0] + m[1] * v[1] + m[2] * v[2]
        mag = b[0] * b[0] + b[1] * b[1] + b[2] * b[2]
        energy = p * (1.0 / (GAMMA - 1.0)) + 0.5 * (kin + mag)
        for k, value in enumerate([rho, *m, *b, energy]):
            u0[k, i] = value
        prim = [rho, *v, *b, p]
        put_primitive(i, prim)

    def merged(i, ref, k):
        back = pltpu.roll(patch[k], jnp.bitwise_and(wide - 2 - 4 * i, wide - 1), 2)
        return ref[k, i] + jnp.where(inside, 0.0, back)

    def middle_row(i):
        u = [merged(i, u1, k) for k in range(8)]
        for k in range(8):
            u1[k, i] = u[k]
        prim = to_primitive(u)
        put_primitive(i, prim)

    def final_row(i):
        for k in range(8):
            value = merged(i, u0, k)
            for z in range(2):
                out_ref[k, i, pl.ds(z, half, stride=2), :] = value[z]

    def z_up(x):
        return jnp.stack([x[1], pltpu.roll(x[0], half - 1, 0)])

    def z_down(x):
        return jnp.stack([pltpu.roll(x[1], 1, 0), x[0]])

    def y_up(x):
        return pltpu.roll(x, wide - 1, 2)

    def y_down(x):
        return pltpu.roll(x, 1, 2)

    def periodic(whole, halved, n, up, down):
        left, right = [], []
        for k in range(8):
            d = up(halved[k]) - halved[k]
            h = limited(d, down(d))
            left.append(whole[k] + h)
            right.append(up(whole[k] - h))
        face = face_flux(left, right, n)
        return [f - down(f) for f in face]

    def x_face(i):
        left, right = [], []
        for k in range(8):
            d = wh[k, i + 4] - wh[k, i + 3]
            h = limited(d, sd[k])
            here = w[k, i + 3]
            left.append(sl[k])
            right.append(here - h)
            sd[k] = d
            sl[k] = here + h
        return face_flux(left, right, 0)

    def x_begin(i):
        for k in range(8):
            before = wh[k, i + 1] - wh[k, i]
            d = wh[k, i + 2] - wh[k, i + 1]
            sd[k] = d
            sl[k] = w[k, i + 1] + limited(d, before)
        face = x_face(i - 1)
        for k in range(8):
            sf[k] = face[k]

    def main_row(sec, i, carry):
        whole = [w[k, i + 2] for k in range(8)]
        halved = [wh[k, i + 2] for k in range(8)]
        dz = periodic(whole, halved, 2, z_up, z_down)
        dy = periodic(whole, halved, 1, y_up, y_down)
        fx = x_face(i)
        change = []
        for k in range(8):
            change.append((dz[k] + jnp.where(inside, dy[k], 0.0)) + (fx[k] - sf[k]))
            sf[k] = fx[k]
        ref = u1 if sec else u0
        u = [ref[k, i] for k in range(8)]
        step = 0.5 * TIME_STEP if sec else TIME_STEP
        r = radial(i)
        pull = (2.0 * SHEAR_Q * omega * omega * step) * r
        source = {
            1: (2.0 * omega * step) * u[2] + pull * u[0],
            2: (-2.0 * omega * step) * u[1],
            7: pull * u[1],
        }
        for k in range(8):
            base = 0.5 * (u0[k, i] + u[k]) if sec else u[k]
            value = base - (0.5 * step) * change[k]
            if k in source:
                value = value + source[k]
            (u0 if sec else u1)[k, i] = value
        return carry

    def edge_patch(sec):
        step = 0.5 * TIME_STEP if sec else TIME_STEP

        def turned(x, by):
            return x if by % wide == 0 else pltpu.roll(x, by % wide, 2)

        def rates(low, high, base):
            left, right = [], []
            for k in range(8):
                col = []
                for t in range(-1, 3):
                    start = t - base
                    take = quad < -start
                    if start >= 0:
                        col.append(turned(high[k], -start))
                    elif start == -4:
                        col.append(low[k])
                    elif start < -4:
                        col.append(turned(low[k], -4 - start))
                    else:
                        col.append(jnp.where(take, turned(low[k], -4 - start), turned(high[k], -start)))
                d = [0.5 * (col[t + 1] - col[t]) for t in range(3)]
                left.append(col[1] + limited(d[1], d[0]))
                right.append(col[2] - limited(d[2], d[1]))
            face = face_flux(left, right, 1)
            return [f - pltpu.roll(f, 1, 2) for f in face]

        low_side = rates([yg[sec, 0, k] for k in range(8)], [pack[sec, 0, k] for k in range(8)], 2)
        high_side = rates([pack[sec, 1, k] for k in range(8)], [yg[sec, 1, k] for k in range(8)], 4)
        for k in range(8):
            both = jnp.where(quad < 2, pltpu.roll(high_side[k], wide - 2, 2), low_side[k])
            patch[k] = (-0.5 * step) * both

    shift = shift_ref[0]
    weight = weight_ref[0].astype(jnp.float32) * WEIGHT_SCALE
    out_shift = jnp.where(first, total_y - 1 - shift, shift)
    out_weight = jnp.where(first, 1.0 - weight, weight)

    def gather_copy(sec, step):
        out, ring, _, _ = spread[sec]
        to = peer(step)
        return remote(out.at[to], ring.at[gy], ss.at[sec, 0], sr.at[sec, 0], gx, to)

    def hand_copy(sec, step):
        _, _, back, got = spread[sec]
        to = peer(step)
        return remote(back.at[to], got.at[gy], ss.at[sec, 1], sr.at[sec, 1], other, to)

    def all_gathered(sec):
        out, ring, _, _ = spread[sec]
        few = pl.ds(0, ny - 1)
        return remote(out.at[few], ring.at[few], ss.at[sec, 0], sr.at[sec, 0], gx, north)

    def all_handed(sec):
        _, _, back, got = spread[sec]
        return remote(back, got, ss.at[sec, 1], sr.at[sec, 1], other, gy)

    def parts(q):
        return q // 4, q // 2 % 2, q % 2

    def chain_start(sec, u):
        out, ring, _, _ = spread[sec]

        def fill(row):
            for q in range(32):
                k, j, z = parts(q)
                out[q // share, q % share] = u[k, row + j, z]

        pl.when(first)(lambda: fill(0))
        pl.when(last)(lambda: fill(rows - 2))

        @pl.when(edge)
        def _():
            ring[gy] = out[gy]
            each(1, ny, lambda step: gather_copy(sec, step).start())

    def chain_middle(sec):
        @pl.when(edge)
        def _():
            _, ring, back, _ = spread[sec]
            all_gathered(sec).wait_recv()
            blocks = lax.div(out_shift, wide)
            inner = lax.rem(out_shift, wide)
            src = lax.broadcasted_iota(jnp.int32, (wide, wide), 0)
            dst = lax.broadcasted_iota(jnp.int32, (wide, wide), 1)
            gap = dst - src - inner
            near = jnp.where(gap == 0, 1.0 - out_weight, 0.0) + jnp.where(gap == 1, out_weight, 0.0)
            far = jnp.where(gap == -wide, 1.0 - out_weight, 0.0) + jnp.where(gap == 1 - wide, out_weight, 0.0)

            def times(offset, m):
                x = jnp.stack([ring[lax.rem(j + 2 * ny - offset - blocks, ny)] for j in range(ny)])
                x = x.reshape(32 * half, wide)
                return jnp.dot(x, m, precision=lax.Precision.HIGHEST, preferred_element_type=jnp.float32)

            back[...] = (times(0, near) + times(1, far)).reshape(ny, share, half, wide)
            each(0, ny, lambda step: hand_copy(sec, step).start())

    def chain_end(sec):
        @pl.when(edge)
        def _():
            got = spread[sec][3]
            all_handed(sec).wait_recv()
            delta = jnp.where(first, 1.0, -1.0)
            start = jnp.where(first, 0, rows + 2)
            for j in range(2):
                u = []
                for k in range(8):
                    at = [4 * k + 2 * j + z for z in range(2)]
                    u.append(jnp.stack([got[q // share, q % share] for q in at]))
                momentum = u[2] + u[0] * delta
                u[7] = u[7] + u[2] * delta + 0.5 * u[0]
                u[2] = momentum
                put_primitive(start + j - 2, to_primitive(u))

    def x_copy(sec, side, incoming):
        away = gx - 1 if side == 0 else gx + 1
        own = w.at[:, 2:4] if side == 0 else w.at[:, rows : rows + 2]
        slot = side if incoming else 1 - side
        return remote(own, xg.at[sec, slot], xs.at[sec, side], xr.at[sec, slot], away, gy)

    def y_copy(sec, side, incoming):
        away = south if side == 0 else north
        slot = side if incoming else 1 - side
        return remote(pack.at[sec, side], yg.at[sec, slot], ys.at[sec, side], yr.at[sec, slot], gx, away)

    def on_side(side, do):
        pl.when(gx > 0 if side == 0 else gx < nx - 1)(do)

    for load in loads:
        load.wait()
    for sec in range(2):
        one_row = middle_row if sec else start_row

        def two_rows(t, carry):
            one_row(2 * t)
            one_row(2 * t + 1)
            return carry

        def outer_rows(t, carry):
            return two_rows(t * (rows // 2 - 1), carry)

        lax.fori_loop(0, 2, outer_rows, 0)
        if sec == 0:
            await_greetings()
        chain_start(sec, u1 if sec else u0)
        for side in range(2):
            on_side(side, lambda: x_copy(sec, side, False).start())
        lax.fori_loop(1, rows // 2 - 1, two_rows, 0)
        store_packs(sec)
        x_begin(2)
        for side in range(2):
            y_copy(sec, side, False).start()
        row = functools.partial(main_row, sec)
        cut = min(CUT * rows // 32, rows - 2)
        lax.fori_loop(2, cut, row, 0)
        chain_middle(sec)
        lax.fori_loop(cut, rows - 2, row, 0)
        for side in range(2):
            y_copy(sec, side, True).wait_recv()
        edge_patch(sec)
        for side in range(2):

            def take():
                x_copy(sec, side, True).wait_recv()
                for k in range(8):
                    value = xg[sec, side, k]
                    start = 0 if side == 0 else rows + 2
                    w[k, start : start + 2] = value
                    wh[k, start : start + 2] = 0.5 * value

            on_side(side, take)
        chain_end(sec)
        lax.fori_loop(rows - 2, rows, row, 0)
        x_begin(0)
        lax.fori_loop(0, 2, row, 0)
        for side in range(2):
            on_side(side, lambda: x_copy(sec, side, False).wait_send())
            y_copy(sec, side, False).wait_send()
    each(0, rows // 2, lambda t: (final_row(2 * t), final_row(2 * t + 1)))

    @pl.when(edge)
    def _():
        for sec in range(2):
            all_gathered(sec).wait_send()
            all_handed(sec).wait_send()


def solution(mesh):
    nx, ny = mesh.shape["gx"], mesh.shape["gy"]

    def on_device(density, velocity, bfield, pressure, shear_shift, remap_weight):
        rows, nz, wide = density.shape
        half = nz // 2
        tile = (2, half, wide)
        slab = (8, 2, *tile)
        f32 = jnp.float32
        dma = pltpu.SemaphoreType.DMA
        vmem = pl.BlockSpec(memory_space=pltpu.VMEM)
        hbm = pl.BlockSpec(memory_space=pltpu.HBM)
        smem = pl.BlockSpec(memory_space=pltpu.SMEM)
        return pl.pallas_call(
            functools.partial(kernel, nx, ny),
            out_shape=jax.ShapeDtypeStruct((8, rows, nz, wide), f32),
            in_specs=[smem, smem, hbm, hbm, hbm, hbm],
            out_specs=vmem,
            scratch_shapes=[
                pltpu.VMEM((rows, nz, wide), f32),
                pltpu.VMEM((3, rows, nz, wide), f32),
                pltpu.VMEM((3, rows, nz, wide), f32),
                pltpu.VMEM((rows, nz, wide), f32),
                pltpu.VMEM((8, rows, *tile), f32),
                pltpu.VMEM((8, rows, *tile), f32),
                pltpu.VMEM((8, rows + 4, *tile), f32),
                pltpu.VMEM((8, rows + 4, *tile), f32),
                pltpu.VMEM((8, *tile), f32),
                pltpu.VMEM((8, *tile), f32),
                pltpu.VMEM((8, *tile), f32),
                pltpu.VMEM((2, 2, 8, *tile), f32),
                pltpu.VMEM((8, *tile), f32),
                pltpu.VMEM((2, 2, *slab), f32),
                pltpu.VMEM((2, 2, 8, *tile), f32),
                *[pltpu.VMEM((ny, 32 // ny, half, wide), f32) for _ in range(8)],
                dma((2, 2)),
                dma((2, 2)),
                dma((2, 2)),
                dma((2, 2)),
                dma((2, 2)),
                dma((2, 2)),
                dma((4,)),
            ],
            compiler_params=pltpu.CompilerParams(
                collective_id=0, has_side_effects=True, vmem_limit_bytes=32 * 1024 * 1024
            ),
        )(shear_shift.reshape(1), remap_weight.reshape(1), density, velocity, bfield, pressure)

    placed = (
        P("gx", None, "gy"),
        P(None, "gx", None, "gy"),
        P(None, "gx", None, "gy"),
        P("gx", None, "gy"),
        P(),
        P(),
    )
    return jax.shard_map(
        on_device, mesh=mesh, in_specs=placed, out_specs=P(None, "gx", None, "gy"), check_vma=False
    )
```

```python
import functools

import jax
import jax.numpy as jnp
from jax import lax
from jax.experimental import pallas as pl
from jax.experimental.pallas import tpu as pltpu
from jax.sharding import PartitionSpec as P

GAMMA = 5.0 / 3.0
SHEAR_Q = 1.5
TIME_STEP = 0.03
WEIGHT_SCALE = 1.0 / 65536.0
TINY = 1e-30
MESH = pl.DeviceIdType.MESH
CUTS = (12, 6, 18)


def limited(upper, lower):
    return jnp.minimum(jnp.maximum(upper, jnp.minimum(lower, 0.0)), jnp.maximum(lower, 0.0))


def side_terms(state, n):
    rho, v, b, p = state[0], state[1:4], state[4:7], state[7]
    a, c = [t for t in range(3) if t != n]
    bn2 = b[n] * b[n]
    bt2 = b[a] * b[a] + b[c] * b[c]
    hb2 = 0.5 * (bt2 + bn2)
    pt = p + hb2
    energy = pt + 0.5 * (p + rho * (v[0] * v[0] + v[1] * v[1] + v[2] * v[2]))
    hgp = (0.5 * GAMMA) * p
    spread = hgp - hb2
    inner = spread * spread + (GAMMA * p) * bt2
    square = (hgp + hb2) + inner * lax.rsqrt(jnp.maximum(inner, TINY))
    fast = square * lax.rsqrt(jnp.maximum(rho * square, TINY))
    return pt - bn2, energy, jnp.abs(v[n]) + fast


def side_flux(state, n, terms, speed):
    rho, v, b = state[0], state[1:4], state[4:7]
    a, c = [t for t in range(3) if t != n]
    stress, energy, _ = terms
    drift = v[n] + speed
    mass = rho * drift
    wa, wc = b[n] * v[a], b[n] * v[c]
    flux = [None] * 8
    flux[0] = mass
    flux[1 + n] = mass * v[n] + stress
    flux[1 + a] = mass * v[a] - b[n] * b[a]
    flux[1 + c] = mass * v[c] - b[n] * b[c]
    flux[4 + a] = drift * b[a] - wa
    flux[4 + c] = drift * b[c] - wc
    flux[7] = (energy * drift + stress * v[n]) - (b[a] * wa + b[c] * wc)
    return flux


def face_flux(left, right, n):
    tl, tr = side_terms(left, n), side_terms(right, n)
    speed = jnp.maximum(tl[2], tr[2])
    fl, fr = side_flux(left, n, tl, speed), side_flux(right, n, tr, -speed)
    return [speed * (left[k] - right[k]) if k == 4 + n else fl[k] + fr[k] for k in range(8)]


def to_primitive(u):
    inv = 1.0 / u[0]
    v = [u[k] * inv for k in (1, 2, 3)]
    kin = u[1] * v[0] + u[2] * v[1] + u[3] * v[2]
    mag = u[4] * u[4] + u[5] * u[5] + u[6] * u[6]
    return [u[0], *v, u[4], u[5], u[6], (GAMMA - 1.0) * (u[7] - 0.5 * (kin + mag))]


def kernel(
    nx, ny, shift_ref, weight_ref, rho_in, vel_in, mag_in, pre_in, out_ref, rho_ref, vel_ref, mag_ref, pre_ref,
    u0, u1, w0, wh0, w1, wh1, sd0, sl0, sf0, sd1, sl1, sf1, pack, patch, xg, yg, out0, ring0, back0, got0, out1, ring1, back1, got1,
    xs, xr, ys, yr, ss, sr, ls,
):
    rows, nz, wide = rho_ref.shape
    half = nz // 2
    total_x = nx * rows
    total_y = ny * wide
    omega = 1.0 / (SHEAR_Q * total_x)
    share = 32 // ny
    prims, halves = (w0, w1), (wh0, wh1)
    carried = ((sd0, sl0, sf0), (sd1, sl1, sf1))
    spread = ((out0, ring0, back0, got0), (out1, ring1, back1, got1))
    gx = lax.axis_index("gx")
    gy = lax.axis_index("gy")
    first = gx == 0
    last = gx == nx - 1
    edge = jnp.logical_or(first, last)
    other = jnp.where(first, nx - 1, 0)
    north = lax.rem(gy + 1, ny)
    south = lax.rem(gy + ny - 1, ny)
    lane = lax.broadcasted_iota(jnp.int32, (2, half, wide), 2)
    quad = jnp.bitwise_and(lane, 3)
    even = jnp.bitwise_and(lane, 4) == 0
    inside = jnp.logical_and(lane >= 2, lane < wide - 2)

    loads = [
        pltpu.make_async_copy(src, dst, ls.at[k])
        for k, (src, dst) in enumerate(
            [(rho_in, rho_ref), (vel_in, vel_ref), (mag_in, mag_ref), (pre_in, pre_ref)]
        )
    ]
    for load in loads:
        load.start()

    barrier = pltpu.get_barrier_semaphore()

    def greet(x, y):
        pl.semaphore_signal(barrier, inc=1, device_id=(x, y), device_id_type=MESH)

    greet(gx, north)
    greet(gx, south)

    @pl.when(gx > 0)
    def _():
        greet(gx - 1, gy)

    @pl.when(gx < nx - 1)
    def _():
        greet(gx + 1, gy)

    def each(low, high, do):
        def body(t, carry):
            do(t)
            return carry

        lax.fori_loop(low, high, body, 0)

    def peer(step):
        return lax.rem(gy + step, ny)

    @pl.when(edge)
    def _():
        each(1, ny, lambda step: greet(gx, peer(step)))
        each(0, ny, lambda step: greet(other, peer(step)))

    def await_greetings():
        pl.semaphore_wait(barrier, jnp.where(edge, 2 + 2 * ny, 4))

    def remote(src, dst, send, recv, x, y):
        return pltpu.make_async_remote_copy(
            src_ref=src, dst_ref=dst, send_sem=send, recv_sem=recv, device_id=(x, y), device_id_type=MESH
        )

    def radial(i):
        return (gx * rows + i).astype(jnp.float32) + (0.5 - 0.5 * total_x)

    def put_primitive(sec, i, prim):
        for k in range(8):
            prims[sec][k, i + 2] = prim[k]
            halves[sec][k, i + 2] = 0.5 * prim[k]

    def store_packs(sec):
        def some(t, carry):
            for k in (2 * t, 2 * t + 1):
                both = []
                for odd in range(2):
                    acc = jnp.zeros((2, half, wide), jnp.float32)
                    slot = lax.shift_right_logical(jnp.bitwise_and(lane - 4 * odd, wide - 1), 3)
                    for i in range(odd, rows, 2):
                        moved = pltpu.roll(prims[sec][k, i + 2], (4 * i + 4) % wide, 2)
                        acc = jnp.where(slot == i // 2, moved, acc)
                    both.append(acc)
                pack[sec, 0, k] = pltpu.roll(jnp.where(even, both[1], both[0]), wide - 4, 2)
                pack[sec, 1, k] = jnp.where(even, both[0], both[1])
            return carry

        lax.fori_loop(0, 4, some, 0)

    def start_row(i):
        def load(ref, *lead):
            return jnp.stack([ref[(*lead, i, pl.ds(z, half, stride=2), slice(None))] for z in range(2)])

        rho = load(rho_ref)
        v = [load(vel_ref, 0), load(vel_ref, 1) - SHEAR_Q * omega * radial(i), load(vel_ref, 2)]
        b = [load(mag_ref, k) for k in range(3)]
        p = load(pre_ref)
        m = [rho * v[k] for k in range(3)]
        kin = m[0] * v[0] + m[1] * v[1] + m[2] * v[2]
        mag = b[0] * b[0] + b[1] * b[1] + b[2] * b[2]
        energy = p * (1.0 / (GAMMA - 1.0)) + 0.5 * (kin + mag)
        for k, value in enumerate([rho, *m, *b, energy]):
            u0[k, i] = value
        put_primitive(0, i, [rho, *v, *b, p])

    def merged(i, ref, k):
        back = pltpu.roll(patch[k], jnp.bitwise_and(wide - 2 - 4 * i, wide - 1), 2)
        return ref[k, i] + jnp.where(inside, 0.0, back)

    def middle_row(i):
        u = [merged(i, u1, k) for k in range(8)]
        for k in range(8):
            u1[k, i] = u[k]
        put_primitive(1, i, to_primitive(u))

    def final_row(i):
        for k in range(8):
            value = merged(i, u0, k)
            for z in range(2):
                out_ref[k, i, pl.ds(z, half, stride=2), :] = value[z]

    def z_up(x):
        return jnp.stack([x[1], pltpu.roll(x[0], half - 1, 0)])

    def z_down(x):
        return jnp.stack([pltpu.roll(x[1], 1, 0), x[0]])

    def y_up(x):
        return pltpu.roll(x, wide - 1, 2)

    def y_down(x):
        return pltpu.roll(x, 1, 2)

    def periodic(whole, halved, n, up, down):
        left, right = [], []
        for k in range(8):
            d = up(halved[k]) - halved[k]
            h = limited(d, down(d))
            left.append(whole[k] + h)
            right.append(up(whole[k] - h))
        face = face_flux(left, right, n)
        return [f - down(f) for f in face]

    def x_face(sec, i):
        w, wh = prims[sec], halves[sec]
        sd, sl, _ = carried[sec]
        left, right = [], []
        for k in range(8):
            d = wh[k, i + 4] - wh[k, i + 3]
            h = limited(d, sd[k])
            here = w[k, i + 3]
            left.append(sl[k])
            right.append(here - h)
            sd[k] = d
            sl[k] = here + h
        return face_flux(left, right, 0)

    def x_begin(sec, i):
        w, wh = prims[sec], halves[sec]
        sd, sl, sf = carried[sec]
        for k in range(8):
            before = wh[k, i + 1] - wh[k, i]
            d = wh[k, i + 2] - wh[k, i + 1]
            sd[k] = d
            sl[k] = w[k, i + 1] + limited(d, before)
        face = x_face(sec, i - 1)
        for k in range(8):
            sf[k] = face[k]

    def main_row(sec, i, carry):
        sf = carried[sec][2]
        whole = [prims[sec][k, i + 2] for k in range(8)]
        halved = [halves[sec][k, i + 2] for k in range(8)]
        dz = periodic(whole, halved, 2, z_up, z_down)
        dy = periodic(whole, halved, 1, y_up, y_down)
        fx = x_face(sec, i)
        change = []
        for k in range(8):
            change.append((dz[k] + jnp.where(inside, dy[k], 0.0)) + (fx[k] - sf[k]))
            sf[k] = fx[k]
        ref = u1 if sec else u0
        u = [ref[k, i] for k in range(8)]
        step = 0.5 * TIME_STEP if sec else TIME_STEP
        r = radial(i)
        pull = (2.0 * SHEAR_Q * omega * omega * step) * r
        source = {
            1: (2.0 * omega * step) * u[2] + pull * u[0],
            2: (-2.0 * omega * step) * u[1],
            7: pull * u[1],
        }
        for k in range(8):
            base = 0.5 * (u0[k, i] + u[k]) if sec else u[k]
            value = base - (0.5 * step) * change[k]
            if k in source:
                value = value + source[k]
            (u0 if sec else u1)[k, i] = value
        return carry

    def edge_patch(sec):
        step = 0.5 * TIME_STEP if sec else TIME_STEP

        def turned(x, by):
            return x if by % wide == 0 else pltpu.roll(x, by % wide, 2)

        def rates(low, high, base):
            left, right = [], []
            for k in range(8):
                col = []
                for t in range(-1, 3):
                    start = t - base
                    take = quad < -start
                    if start >= 0:
                        col.append(turned(high[k], -start))
                    elif start == -4:
                        col.append(low[k])
                    elif start < -4:
                        col.append(turned(low[k], -4 - start))
                    else:
                        col.append(jnp.where(take, turned(low[k], -4 - start), turned(high[k], -start)))
                d = [0.5 * (col[t + 1] - col[t]) for t in range(3)]
                left.append(col[1] + limited(d[1], d[0]))
                right.append(col[2] - limited(d[2], d[1]))
            face = face_flux(left, right, 1)
            return [f - pltpu.roll(f, 1, 2) for f in face]

        low_side = rates([yg[sec, 0, k] for k in range(8)], [pack[sec, 0, k] for k in range(8)], 2)
        high_side = rates([pack[sec, 1, k] for k in range(8)], [yg[sec, 1, k] for k in range(8)], 4)
        for k in range(8):
            both = jnp.where(quad < 2, pltpu.roll(high_side[k], wide - 2, 2), low_side[k])
            patch[k] = (-0.5 * step) * both

    shift = shift_ref[0]
    weight = weight_ref[0].astype(jnp.float32) * WEIGHT_SCALE
    out_shift = jnp.where(first, total_y - 1 - shift, shift)
    out_weight = jnp.where(first, 1.0 - weight, weight)

    def gather_copy(sec, step):
        out, ring, _, _ = spread[sec]
        to = peer(step)
        return remote(out.at[to], ring.at[gy], ss.at[sec, 0], sr.at[sec, 0], gx, to)

    def hand_copy(sec, step):
        _, _, back, got = spread[sec]
        to = peer(step)
        return remote(back.at[to], got.at[gy], ss.at[sec, 1], sr.at[sec, 1], other, to)

    def all_gathered(sec):
        out, ring, _, _ = spread[sec]
        few = pl.ds(0, ny - 1)
        return remote(out.at[few], ring.at[few], ss.at[sec, 0], sr.at[sec, 0], gx, north)

    def all_handed(sec):
        _, _, back, got = spread[sec]
        return remote(back, got, ss.at[sec, 1], sr.at[sec, 1], other, gy)

    def parts(q):
        return q // 4, q // 2 % 2, q % 2

    def chain_start(sec, u):
        out, ring, _, _ = spread[sec]

        def fill(row):
            for q in range(32):
                k, j, z = parts(q)
                out[q // share, q % share] = u[k, row + j, z]

        pl.when(first)(lambda: fill(0))
        pl.when(last)(lambda: fill(rows - 2))

        @pl.when(edge)
        def _():
            ring[gy] = out[gy]
            each(1, ny, lambda step: gather_copy(sec, step).start())

    def chain_middle(sec):
        @pl.when(edge)
        def _():
            _, ring, back, _ = spread[sec]
            all_gathered(sec).wait_recv()
            blocks = lax.div(out_shift, wide)
            inner = lax.rem(out_shift, wide)
            src = lax.broadcasted_iota(jnp.int32, (wide, wide), 0)
            dst = lax.broadcasted_iota(jnp.int32, (wide, wide), 1)
            gap = dst - src - inner
            near = jnp.where(gap == 0, 1.0 - out_weight, 0.0) + jnp.where(gap == 1, out_weight, 0.0)
            far = jnp.where(gap == -wide, 1.0 - out_weight, 0.0) + jnp.where(gap == 1 - wide, out_weight, 0.0)

            def times(offset, m):
                x = jnp.stack([ring[lax.rem(j + 2 * ny - offset - blocks, ny)] for j in range(ny)])
                x = x.reshape(32 * half, wide)
                return jnp.dot(x, m, precision=lax.Precision.HIGHEST, preferred_element_type=jnp.float32)

            back[...] = (times(0, near) + times(1, far)).reshape(ny, share, half, wide)
            each(0, ny, lambda step: hand_copy(sec, step).start())

    def chain_end(sec):
        @pl.when(edge)
        def _():
            got = spread[sec][3]
            all_handed(sec).wait_recv()
            delta = jnp.where(first, 1.0, -1.0)
            start = jnp.where(first, 0, rows + 2)
            for j in range(2):
                u = []
                for k in range(8):
                    at = [4 * k + 2 * j + z for z in range(2)]
                    u.append(jnp.stack([got[q // share, q % share] for q in at]))
                momentum = u[2] + u[0] * delta
                u[7] = u[7] + u[2] * delta + 0.5 * u[0]
                u[2] = momentum
                put_primitive(sec, start + j - 2, to_primitive(u))

    def x_copy(sec, side, incoming):
        away = gx - 1 if side == 0 else gx + 1
        w = prims[sec]
        own = w.at[:, 2:4] if side == 0 else w.at[:, rows : rows + 2]
        slot = side if incoming else 1 - side
        return remote(own, xg.at[sec, slot], xs.at[sec, side], xr.at[sec, slot], away, gy)

    def y_copy(sec, side, incoming):
        away = south if side == 0 else north
        slot = side if incoming else 1 - side
        return remote(pack.at[sec, side], yg.at[sec, slot], ys.at[sec, side], yr.at[sec, slot], gx, away)

    def on_side(side, do):
        pl.when(gx > 0 if side == 0 else gx < nx - 1)(do)

    def two_rows(sec):
        one_row = middle_row if sec else start_row

        def body(t):
            one_row(2 * t)
            one_row(2 * t + 1)

        return body

    def outer_rows(sec):
        each(0, 2, lambda t: two_rows(sec)(t * (rows // 2 - 1)))
        if sec == 0:
            await_greetings()
        chain_start(sec, u1 if sec else u0)
        for side in range(2):
            on_side(side, lambda: x_copy(sec, side, False).start())

    def send_columns(sec):
        store_packs(sec)
        for side in range(2):
            y_copy(sec, side, False).start()

    def take_columns(sec):
        for side in range(2):
            y_copy(sec, side, True).wait_recv()
        edge_patch(sec)

    def take_rows(sec):
        for side in range(2):

            def take():
                x_copy(sec, side, True).wait_recv()
                start = 0 if side == 0 else rows + 2
                for k in range(8):
                    value = xg[sec, side, k]
                    prims[sec][k, start : start + 2] = value
                    halves[sec][k, start : start + 2] = 0.5 * value

            on_side(side, take)
        chain_end(sec)

    def sent(sec):
        for side in range(2):
            on_side(side, lambda: x_copy(sec, side, False).wait_send())
            y_copy(sec, side, False).wait_send()

    def main(sec, low, high):
        lax.fori_loop(low, high, functools.partial(main_row, sec), 0)

    cuts = [min(c * rows // 32, rows - 4) for c in CUTS]
    cuts = [cuts[0], max(cuts[1], 4), max(cuts[2], 4)]
    for load in loads:
        load.wait()
    outer_rows(0)
    each(1, rows // 2 - 1, two_rows(0))
    send_columns(0)
    x_begin(0, 2)
    main(0, 2, cuts[0])
    chain_middle(0)
    main(0, cuts[0], rows - 2)
    take_columns(0)
    each(1, rows // 2 - 1, two_rows(1))
    x_begin(1, 4)
    main(1, 4, cuts[1])
    take_rows(0)
    main(0, rows - 2, rows)
    x_begin(0, 0)
    main(0, 0, 2)
    outer_rows(1)
    send_columns(1)
    main(1, cuts[1], cuts[2])
    chain_middle(1)
    main(1, cuts[2], rows - 2)
    take_columns(1)
    take_rows(1)
    main(1, rows - 2, rows)
    x_begin(1, 0)
    main(1, 0, 4)
    sent(0)
    sent(1)
    each(0, rows // 2, lambda t: (final_row(2 * t), final_row(2 * t + 1)))

    @pl.when(edge)
    def _():
        for sec in range(2):
            all_gathered(sec).wait_send()
            all_handed(sec).wait_send()


def solution(mesh):
    nx, ny = mesh.shape["gx"], mesh.shape["gy"]

    def on_device(density, velocity, bfield, pressure, shear_shift, remap_weight):
        rows, nz, wide = density.shape
        half = nz // 2
        tile = (2, half, wide)
        slab = (8, 2, *tile)
        f32 = jnp.float32
        dma = pltpu.SemaphoreType.DMA
        vmem = pl.BlockSpec(memory_space=pltpu.VMEM)
        hbm = pl.BlockSpec(memory_space=pltpu.HBM)
        smem = pl.BlockSpec(memory_space=pltpu.SMEM)
        return pl.pallas_call(
            functools.partial(kernel, nx, ny),
            out_shape=jax.ShapeDtypeStruct((8, rows, nz, wide), f32),
            in_specs=[smem, smem, hbm, hbm, hbm, hbm],
            out_specs=vmem,
            scratch_shapes=[
                pltpu.VMEM((rows, nz, wide), f32),
                pltpu.VMEM((3, rows, nz, wide), f32),
                pltpu.VMEM((3, rows, nz, wide), f32),
                pltpu.VMEM((rows, nz, wide), f32),
                pltpu.VMEM((8, rows, *tile), f32),
                pltpu.VMEM((8, rows, *tile), f32),
                *[pltpu.VMEM((8, rows + 4, *tile), f32) for _ in range(4)],
                *[pltpu.VMEM((8, *tile), f32) for _ in range(6)],
                pltpu.VMEM((2, 2, 8, *tile), f32),
                pltpu.VMEM((8, *tile), f32),
                pltpu.VMEM((2, 2, *slab), f32),
                pltpu.VMEM((2, 2, 8, *tile), f32),
                *[pltpu.VMEM((ny, 32 // ny, half, wide), f32) for _ in range(8)],
                dma((2, 2)),
                dma((2, 2)),
                dma((2, 2)),
                dma((2, 2)),
                dma((2, 2)),
                dma((2, 2)),
                dma((4,)),
            ],
            compiler_params=pltpu.CompilerParams(
                collective_id=0, has_side_effects=True, vmem_limit_bytes=32 * 1024 * 1024
            ),
        )(
            shear_shift.reshape(1),
            remap_weight.reshape(1),
            *[
                pltpu.with_memory_space_constraint(x, pltpu.HBM)
                for x in (density, velocity, bfield, pressure)
            ],
        )

    placed = (
        P("gx", None, "gy"),
        P(None, "gx", None, "gy"),
        P(None, "gx", None, "gy"),
        P("gx", None, "gy"),
        P(),
        P(),
    )
    return jax.shard_map(
        on_device, mesh=mesh, in_specs=placed, out_specs=P(None, "gx", None, "gy"), check_vma=False
    )
```

```python
import functools

import jax
import jax.numpy as jnp
from jax import lax
from jax.experimental import pallas as pl
from jax.experimental.pallas import tpu as pltpu
from jax.sharding import PartitionSpec as P

GAMMA = 5.0 / 3.0
SHEAR_Q = 1.5
TIME_STEP = 0.03
WEIGHT_SCALE = 1.0 / 65536.0
TINY = 1e-30
MESH = pl.DeviceIdType.MESH
CUTS = (4, 14, 6, 16)


def limited(upper, lower):
    return jnp.minimum(jnp.maximum(upper, jnp.minimum(lower, 0.0)), jnp.maximum(lower, 0.0))


def side_terms(state, n):
    rho, v, b, p = state[0], state[1:4], state[4:7], state[7]
    a, c = [t for t in range(3) if t != n]
    bn2 = b[n] * b[n]
    bt2 = b[a] * b[a] + b[c] * b[c]
    hb2 = 0.5 * (bt2 + bn2)
    pt = p + hb2
    energy = pt + 0.5 * (p + rho * (v[0] * v[0] + v[1] * v[1] + v[2] * v[2]))
    hgp = (0.5 * GAMMA) * p
    spread = hgp - hb2
    inner = spread * spread + (GAMMA * p) * bt2
    square = (hgp + hb2) + inner * lax.rsqrt(jnp.maximum(inner, TINY))
    fast = square * lax.rsqrt(jnp.maximum(rho * square, TINY))
    return pt - bn2, energy, jnp.abs(v[n]) + fast


def side_flux(state, n, terms, speed):
    rho, v, b = state[0], state[1:4], state[4:7]
    a, c = [t for t in range(3) if t != n]
    stress, energy, _ = terms
    drift = v[n] + speed
    mass = rho * drift
    wa, wc = b[n] * v[a], b[n] * v[c]
    flux = [None] * 8
    flux[0] = mass
    flux[1 + n] = mass * v[n] + stress
    flux[1 + a] = mass * v[a] - b[n] * b[a]
    flux[1 + c] = mass * v[c] - b[n] * b[c]
    flux[4 + a] = drift * b[a] - wa
    flux[4 + c] = drift * b[c] - wc
    flux[7] = (energy * drift + stress * v[n]) - (b[a] * wa + b[c] * wc)
    return flux


def face_flux(left, right, n):
    tl, tr = side_terms(left, n), side_terms(right, n)
    speed = jnp.maximum(tl[2], tr[2])
    fl, fr = side_flux(left, n, tl, speed), side_flux(right, n, tr, -speed)
    return [speed * (left[k] - right[k]) if k == 4 + n else fl[k] + fr[k] for k in range(8)]


def to_primitive(u):
    inv = 1.0 / u[0]
    v = [u[k] * inv for k in (1, 2, 3)]
    kin = u[1] * v[0] + u[2] * v[1] + u[3] * v[2]
    mag = u[4] * u[4] + u[5] * u[5] + u[6] * u[6]
    return [u[0], *v, u[4], u[5], u[6], (GAMMA - 1.0) * (u[7] - 0.5 * (kin + mag))]


def kernel(
    nx, ny, shift_ref, weight_ref, rho_in, vel_in, mag_in, pre_in, out_ref, rho_ref, vel_ref, mag_ref, pre_ref,
    u0, u1, w0, wh0, w1, wh1, ylo, yhi, sd0, sl0, sf0, sd1, sl1, sf1, pack, patch, xg, yg, out0, ring0, back0, got0, out1, ring1, back1, got1,
    xs, xr, ys, yr, ss, sr, ls,
):
    rows, nz, wide = rho_ref.shape
    half = nz // 2
    total_x = nx * rows
    total_y = ny * wide
    omega = 1.0 / (SHEAR_Q * total_x)
    share = 32 // ny
    prims, halves = (w0, w1), (wh0, wh1)
    carried = ((sd0, sl0, sf0), (sd1, sl1, sf1))
    spread = ((out0, ring0, back0, got0), (out1, ring1, back1, got1))
    gx = lax.axis_index("gx")
    gy = lax.axis_index("gy")
    first = gx == 0
    last = gx == nx - 1
    edge = jnp.logical_or(first, last)
    other = jnp.where(first, nx - 1, 0)
    north = lax.rem(gy + 1, ny)
    south = lax.rem(gy + ny - 1, ny)
    lane = lax.broadcasted_iota(jnp.int32, (2, half, wide), 2)
    quad = jnp.bitwise_and(lane, 3)
    even = jnp.bitwise_and(lane, 4) == 0
    inside = jnp.logical_and(lane >= 2, lane < wide - 2)

    loads = [
        pltpu.make_async_copy(src, dst, ls.at[k])
        for k, (src, dst) in enumerate(
            [(rho_in, rho_ref), (vel_in, vel_ref), (mag_in, mag_ref), (pre_in, pre_ref)]
        )
    ]
    for load in loads:
        load.start()

    barrier = pltpu.get_barrier_semaphore()

    def greet(x, y):
        pl.semaphore_signal(barrier, inc=1, device_id=(x, y), device_id_type=MESH)

    greet(gx, north)
    greet(gx, south)

    @pl.when(gx > 0)
    def _():
        greet(gx - 1, gy)

    @pl.when(gx < nx - 1)
    def _():
        greet(gx + 1, gy)

    def to_all(low, do):
        for step in range(low, ny):
            do(step)

    def each(low, high, do):
        def body(t, carry):
            do(t)
            return carry

        lax.fori_loop(low, high, body, 0)

    def peer(step):
        return jnp.bitwise_and(gy + step, ny - 1)

    @pl.when(edge)
    def _():
        to_all(1, lambda step: greet(gx, peer(step)))
        greet(other, gy)

    def await_greetings():
        pl.semaphore_wait(barrier, jnp.where(edge, 3 + ny, 4))

    def remote(src, dst, send, recv, x, y):
        return pltpu.make_async_remote_copy(
            src_ref=src, dst_ref=dst, send_sem=send, recv_sem=recv, device_id=(x, y), device_id_type=MESH
        )

    def radial(i):
        return (gx * rows + i).astype(jnp.float32) + (0.5 - 0.5 * total_x)

    def put_primitive(sec, i, prim):
        for k in range(8):
            prims[sec][k, i + 2] = prim[k]
            halves[sec][k, i + 2] = 0.5 * prim[k]

    def store_packs(sec):
        def some(t, carry):
            for k in [4 * t + j for j in range(4)]:
                both = []
                for odd in range(2):
                    acc = jnp.zeros((2, half, wide), jnp.float32)
                    slot = lax.shift_right_logical(jnp.bitwise_and(lane - 4 * odd, wide - 1), 3)
                    for i in range(odd, rows, 2):
                        moved = pltpu.roll(prims[sec][k, i + 2], (4 * i + 4) % wide, 2)
                        acc = jnp.where(slot == i // 2, moved, acc)
                    both.append(acc)
                pack[sec, 0, k] = pltpu.roll(jnp.where(even, both[1], both[0]), wide - 4, 2)
                pack[sec, 1, k] = jnp.where(even, both[0], both[1])
            return carry

        lax.fori_loop(0, 2, some, 0)

    def y_states(i, prim):
        for k in range(8):
            half_prim = 0.5 * prim[k]
            d = y_up(half_prim) - half_prim
            h = limited(d, y_down(d))
            ylo[k, i] = prim[k] + h
            yhi[k, i] = y_up(prim[k] - h)

    def start_row(i):
        def load(ref, *lead):
            return jnp.stack([ref[(*lead, i, pl.ds(z, half, stride=2), slice(None))] for z in range(2)])

        rho = load(rho_ref)
        v = [load(vel_ref, 0), load(vel_ref, 1) - SHEAR_Q * omega * radial(i), load(vel_ref, 2)]
        b = [load(mag_ref, k) for k in range(3)]
        p = load(pre_ref)
        m = [rho * v[k] for k in range(3)]
        kin = m[0] * v[0] + m[1] * v[1] + m[2] * v[2]
        mag = b[0] * b[0] + b[1] * b[1] + b[2] * b[2]
        energy = p * (1.0 / (GAMMA - 1.0)) + 0.5 * (kin + mag)
        for k, value in enumerate([rho, *m, *b, energy]):
            u0[k, i] = value
        prim = [rho, *v, *b, p]
        put_primitive(0, i, prim)
        y_states(i, prim)

    def merged(i, ref, k):
        back = pltpu.roll(patch[k], jnp.bitwise_and(wide - 2 - 4 * i, wide - 1), 2)
        return ref[k, i] + jnp.where(inside, 0.0, back)

    def middle_row(i):
        u = [merged(i, u1, k) for k in range(8)]
        for k in range(8):
            u1[k, i] = u[k]
        prim = to_primitive(u)
        put_primitive(1, i, prim)
        y_states(i, prim)

    def final_row(i):
        for k in range(8):
            value = merged(i, u0, k)
            for z in range(2):
                out_ref[k, i, pl.ds(z, half, stride=2), :] = value[z]

    def z_up(x):
        return jnp.stack([x[1], pltpu.roll(x[0], half - 1, 0)])

    def z_down(x):
        return jnp.stack([pltpu.roll(x[1], 1, 0), x[0]])

    def y_up(x):
        return pltpu.roll(x, wide - 1, 2)

    def y_down(x):
        return pltpu.roll(x, 1, 2)

    def z_change(whole, halved):
        left, right = [], []
        for k in range(8):
            d = z_up(halved[k]) - halved[k]
            h = limited(d, z_down(d))
            left.append(whole[k] + h)
            right.append(z_up(whole[k] - h))
        face = face_flux(left, right, 2)
        return [f - z_down(f) for f in face]

    def x_face(sec, i):
        w, wh = prims[sec], halves[sec]
        sd, sl, _ = carried[sec]
        left, right = [], []
        for k in range(8):
            d = wh[k, i + 4] - wh[k, i + 3]
            h = limited(d, sd[k])
            here = w[k, i + 3]
            left.append(sl[k])
            right.append(here - h)
            sd[k] = d
            sl[k] = here + h
        return face_flux(left, right, 0)

    def x_begin(sec, i):
        w, wh = prims[sec], halves[sec]
        sd, sl, sf = carried[sec]
        for k in range(8):
            before = wh[k, i + 1] - wh[k, i]
            d = wh[k, i + 2] - wh[k, i + 1]
            sd[k] = d
            sl[k] = w[k, i + 1] + limited(d, before)
        face = x_face(sec, i - 1)
        for k in range(8):
            sf[k] = face[k]

    def main_row(sec, i, carry):
        sf = carried[sec][2]
        whole = [prims[sec][k, i + 2] for k in range(8)]
        halved = [halves[sec][k, i + 2] for k in range(8)]
        dz = z_change(whole, halved)
        fy = face_flux([ylo[k, i] for k in range(8)], [yhi[k, i] for k in range(8)], 1)
        dy = [f - y_down(f) for f in fy]
        fx = x_face(sec, i)
        change = []
        for k in range(8):
            change.append((dz[k] + jnp.where(inside, dy[k], 0.0)) + (fx[k] - sf[k]))
            sf[k] = fx[k]
        ref = u1 if sec else u0
        u = [ref[k, i] for k in range(8)]
        step = 0.5 * TIME_STEP if sec else TIME_STEP
        r = radial(i)
        pull = (2.0 * SHEAR_Q * omega * omega * step) * r
        source = {
            1: (2.0 * omega * step) * u[2] + pull * u[0],
            2: (-2.0 * omega * step) * u[1],
            7: pull * u[1],
        }
        for k in range(8):
            base = 0.5 * (u0[k, i] + u[k]) if sec else u[k]
            value = base - (0.5 * step) * change[k]
            if k in source:
                value = value + source[k]
            (u0 if sec else u1)[k, i] = value
        return carry

    def edge_patch(sec):
        step = 0.5 * TIME_STEP if sec else TIME_STEP

        def turned(x, by):
            return x if by % wide == 0 else pltpu.roll(x, by % wide, 2)

        def rates(low, high, base):
            left, right = [], []
            for k in range(8):
                col = []
                for t in range(-1, 3):
                    start = t - base
                    take = quad < -start
                    if start >= 0:
                        col.append(turned(high[k], -start))
                    elif start == -4:
                        col.append(low[k])
                    elif start < -4:
                        col.append(turned(low[k], -4 - start))
                    else:
                        col.append(jnp.where(take, turned(low[k], -4 - start), turned(high[k], -start)))
                d = [0.5 * (col[t + 1] - col[t]) for t in range(3)]
                left.append(col[1] + limited(d[1], d[0]))
                right.append(col[2] - limited(d[2], d[1]))
            face = face_flux(left, right, 1)
            return [f - pltpu.roll(f, 1, 2) for f in face]

        low_side = rates([yg[sec, 0, k] for k in range(8)], [pack[sec, 0, k] for k in range(8)], 2)
        high_side = rates([pack[sec, 1, k] for k in range(8)], [yg[sec, 1, k] for k in range(8)], 4)
        for k in range(8):
            both = jnp.where(quad < 2, pltpu.roll(high_side[k], wide - 2, 2), low_side[k])
            patch[k] = (-0.5 * step) * both

    shift = shift_ref[0]
    weight = weight_ref[0].astype(jnp.float32) * WEIGHT_SCALE
    out_shift = jnp.where(first, total_y - 1 - shift, shift)
    out_weight = jnp.where(first, 1.0 - weight, weight)

    def gather_copy(sec, step):
        out, ring, _, _ = spread[sec]
        to = peer(step)
        return remote(out.at[to], ring.at[gy], ss.at[sec, 0], sr.at[sec, 0], gx, to)

    def hand_copy(sec, step):
        _, _, back, got = spread[sec]
        to = peer(step)
        return remote(back.at[to], got.at[gy], ss.at[sec, 1], sr.at[sec, 1], other, to)

    def all_gathered(sec):
        out, ring, _, _ = spread[sec]
        few = pl.ds(0, ny - 1)
        return remote(out.at[few], ring.at[few], ss.at[sec, 0], sr.at[sec, 0], gx, north)

    def all_handed(sec):
        _, _, back, got = spread[sec]
        return remote(back, got, ss.at[sec, 1], sr.at[sec, 1], other, gy)

    def parts(q):
        return q // 4, q // 2 % 2, q % 2

    def chain_start(sec, u):
        out, ring, _, _ = spread[sec]

        def fill(row):
            for q in range(32):
                k, j, z = parts(q)
                out[q // share, q % share] = u[k, row + j, z]

        pl.when(first)(lambda: fill(0))
        pl.when(last)(lambda: fill(rows - 2))

        @pl.when(edge)
        def _():
            ring[gy] = out[gy]

    def chain_send(sec):
        @pl.when(edge)
        def _():
            to_all(1, lambda step: gather_copy(sec, step).start())

    def chain_middle(sec):
        @pl.when(edge)
        def _():
            _, ring, back, _ = spread[sec]
            all_gathered(sec).wait_recv()
            blocks = lax.div(out_shift, wide)
            inner = lax.rem(out_shift, wide)
            src = lax.broadcasted_iota(jnp.int32, (wide, wide), 0)
            dst = lax.broadcasted_iota(jnp.int32, (wide, wide), 1)
            gap = dst - src - inner
            near = jnp.where(gap == 0, 1.0 - out_weight, 0.0) + jnp.where(gap == 1, out_weight, 0.0)
            far = jnp.where(gap == -wide, 1.0 - out_weight, 0.0) + jnp.where(gap == 1 - wide, out_weight, 0.0)

            def times(offset, m):
                x = jnp.stack([ring[lax.rem(j + 2 * ny - offset - blocks, ny)] for j in range(ny)])
                x = x.reshape(32 * half, wide)
                return jnp.dot(x, m, precision=lax.Precision.HIGHEST, preferred_element_type=jnp.float32)

            back[...] = (times(0, near) + times(1, far)).reshape(ny, share, half, wide)
            to_all(0, lambda step: hand_copy(sec, step).start())

    def chain_end(sec):
        @pl.when(edge)
        def _():
            got = spread[sec][3]
            all_handed(sec).wait_recv()
            delta = jnp.where(first, 1.0, -1.0)
            start = jnp.where(first, 0, rows + 2)
            for j in range(2):
                u = []
                for k in range(8):
                    at = [4 * k + 2 * j + z for z in range(2)]
                    u.append(jnp.stack([got[q // share, q % share] for q in at]))
                momentum = u[2] + u[0] * delta
                u[7] = u[7] + u[2] * delta + 0.5 * u[0]
                u[2] = momentum
                put_primitive(sec, start + j - 2, to_primitive(u))

    def x_copy(sec, side, incoming):
        away = gx - 1 if side == 0 else gx + 1
        w = prims[sec]
        own = w.at[:, 2:4] if side == 0 else w.at[:, rows : rows + 2]
        slot = side if incoming else 1 - side
        return remote(own, xg.at[sec, slot], xs.at[sec, side], xr.at[sec, slot], away, gy)

    def y_copy(sec, side, incoming):
        away = south if side == 0 else north
        slot = side if incoming else 1 - side
        return remote(pack.at[sec, side], yg.at[sec, slot], ys.at[sec, side], yr.at[sec, slot], gx, away)

    def on_side(side, do):
        pl.when(gx > 0 if side == 0 else gx < nx - 1)(do)

    def some_rows(sec, listed):
        for i in listed:
            (middle_row if sec else start_row)(i)

    def outer_rows(sec):
        some_rows(sec, (0, 1, rows - 2, rows - 1))

    def inner_rows(sec):
        each(0, rows // 4 - 1, lambda t: some_rows(sec, [4 * t + 2 + j for j in range(4)]))

    def send_rows(sec):
        chain_send(sec)
        for side in range(2):
            on_side(side, lambda: x_copy(sec, side, False).start())

    def send_columns(sec):
        for side in range(2):
            y_copy(sec, side, False).start()

    def take_columns(sec):
        for side in range(2):
            y_copy(sec, side, True).wait_recv()
        edge_patch(sec)

    def take_rows(sec):
        for side in range(2):

            def take():
                x_copy(sec, side, True).wait_recv()
                start = 0 if side == 0 else rows + 2
                for k in range(8):
                    value = xg[sec, side, k]
                    prims[sec][k, start : start + 2] = value
                    halves[sec][k, start : start + 2] = 0.5 * value

            on_side(side, take)
        chain_end(sec)

    def sent(sec):
        for side in range(2):
            on_side(side, lambda: x_copy(sec, side, False).wait_send())
            y_copy(sec, side, False).wait_send()

    def main(sec, low, high):
        lax.fori_loop(low, high, functools.partial(main_row, sec), 0)

    cuts = [min(max(c * rows // 32, 4), rows - 4) for c in CUTS]
    for load in loads:
        load.wait()
    outer_rows(0)
    inner_rows(0)
    chain_start(0, u0)
    store_packs(0)
    x_begin(0, 2)
    main(0, 2, cuts[0])
    await_greetings()
    send_rows(0)
    send_columns(0)
    main(0, cuts[0], cuts[1])
    chain_middle(0)
    main(0, cuts[1], rows - 2)
    take_columns(0)
    inner_rows(1)
    x_begin(1, 4)
    main(1, 4, cuts[2])
    take_rows(0)
    main(0, rows - 2, rows)
    x_begin(0, 0)
    main(0, 0, 2)
    outer_rows(1)
    chain_start(1, u1)
    send_rows(1)
    store_packs(1)
    send_columns(1)
    main(1, cuts[2], cuts[3])
    chain_middle(1)
    main(1, cuts[3], rows - 2)
    take_columns(1)
    state = [[ref[k] for k in range(8)] for ref in carried[1]]
    for saved, ref in zip(state, carried[0]):
        for k in range(8):
            ref[k] = saved[k]
    x_begin(1, 2)
    main(1, 2, 4)
    each(1, rows // 2 - 1, lambda t: (final_row(2 * t), final_row(2 * t + 1)))
    take_rows(1)
    for saved, ref in zip(carried[0], carried[1]):
        for k in range(8):
            ref[k] = saved[k]
    main(1, rows - 2, rows)
    x_begin(1, 0)
    main(1, 0, 2)
    for i in (0, 1, rows - 2, rows - 1):
        final_row(i)
    sent(0)
    sent(1)

    @pl.when(edge)
    def _():
        for sec in range(2):
            all_gathered(sec).wait_send()
            all_handed(sec).wait_send()


def solution(mesh):
    nx, ny = mesh.shape["gx"], mesh.shape["gy"]

    def on_device(density, velocity, bfield, pressure, shear_shift, remap_weight):
        rows, nz, wide = density.shape
        half = nz // 2
        tile = (2, half, wide)
        slab = (8, 2, *tile)
        f32 = jnp.float32
        dma = pltpu.SemaphoreType.DMA
        vmem = pl.BlockSpec(memory_space=pltpu.VMEM)
        hbm = pl.BlockSpec(memory_space=pltpu.HBM)
        smem = pl.BlockSpec(memory_space=pltpu.SMEM)
        return pl.pallas_call(
            functools.partial(kernel, nx, ny),
            out_shape=jax.ShapeDtypeStruct((8, rows, nz, wide), f32),
            in_specs=[smem, smem, hbm, hbm, hbm, hbm],
            out_specs=vmem,
            scratch_shapes=[
                pltpu.VMEM((rows, nz, wide), f32),
                pltpu.VMEM((3, rows, nz, wide), f32),
                pltpu.VMEM((3, rows, nz, wide), f32),
                pltpu.VMEM((rows, nz, wide), f32),
                pltpu.VMEM((8, rows, *tile), f32),
                pltpu.VMEM((8, rows, *tile), f32),
                *[pltpu.VMEM((8, rows + 4, *tile), f32) for _ in range(4)],
                *[pltpu.VMEM((8, rows, *tile), f32) for _ in range(2)],
                *[pltpu.VMEM((8, *tile), f32) for _ in range(6)],
                pltpu.VMEM((2, 2, 8, *tile), f32),
                pltpu.VMEM((8, *tile), f32),
                pltpu.VMEM((2, 2, *slab), f32),
                pltpu.VMEM((2, 2, 8, *tile), f32),
                *[pltpu.VMEM((ny, 32 // ny, half, wide), f32) for _ in range(8)],
                dma((2, 2)),
                dma((2, 2)),
                dma((2, 2)),
                dma((2, 2)),
                dma((2, 2)),
                dma((2, 2)),
                dma((4,)),
            ],
            compiler_params=pltpu.CompilerParams(
                collective_id=0, has_side_effects=True, vmem_limit_bytes=40 * 1024 * 1024
            ),
        )(
            shear_shift.reshape(1),
            remap_weight.reshape(1),
            *[
                pltpu.with_memory_space_constraint(x, pltpu.HBM)
                for x in (density, velocity, bfield, pressure)
            ],
        )

    placed = (
        P("gx", None, "gy"),
        P(None, "gx", None, "gy"),
        P(None, "gx", None, "gy"),
        P("gx", None, "gy"),
        P(),
        P(),
    )
    return jax.shard_map(
        on_device, mesh=mesh, in_specs=placed, out_specs=P(None, "gx", None, "gy"), check_vma=False
    )
```

```python
import functools

import jax
import jax.numpy as jnp
from jax import lax
from jax.experimental import pallas as pl
from jax.experimental.pallas import tpu as pltpu
from jax.sharding import PartitionSpec as P

GAMMA = 5.0 / 3.0
SHEAR_Q = 1.5
TIME_STEP = 0.03
WEIGHT_SCALE = 1.0 / 65536.0
TINY = 1e-30
MESH = pl.DeviceIdType.MESH
CUTS = (14, 6, 16)


def limited(upper, lower):
    return jnp.minimum(jnp.maximum(upper, jnp.minimum(lower, 0.0)), jnp.maximum(lower, 0.0))


def side_terms(state, n):
    rho, v, b, p = state[0], state[1:4], state[4:7], state[7]
    a, c = [t for t in range(3) if t != n]
    bn2 = b[n] * b[n]
    bt2 = b[a] * b[a] + b[c] * b[c]
    hb2 = 0.5 * (bt2 + bn2)
    pt = p + hb2
    energy = pt + 0.5 * (p + rho * (v[0] * v[0] + v[1] * v[1] + v[2] * v[2]))
    hgp = (0.5 * GAMMA) * p
    spread = hgp - hb2
    inner = spread * spread + (GAMMA * p) * bt2
    square = (hgp + hb2) + inner * lax.rsqrt(jnp.maximum(inner, TINY))
    fast = square * lax.rsqrt(jnp.maximum(rho * square, TINY))
    return pt - bn2, energy, jnp.abs(v[n]) + fast


def side_flux(state, n, terms, speed):
    rho, v, b = state[0], state[1:4], state[4:7]
    a, c = [t for t in range(3) if t != n]
    stress, energy, _ = terms
    drift = v[n] + speed
    mass = rho * drift
    wa, wc = b[n] * v[a], b[n] * v[c]
    flux = [None] * 8
    flux[0] = mass
    flux[1 + n] = mass * v[n] + stress
    flux[1 + a] = mass * v[a] - b[n] * b[a]
    flux[1 + c] = mass * v[c] - b[n] * b[c]
    flux[4 + a] = drift * b[a] - wa
    flux[4 + c] = drift * b[c] - wc
    flux[7] = (energy * drift + stress * v[n]) - (b[a] * wa + b[c] * wc)
    return flux


def face_flux(left, right, n):
    tl, tr = side_terms(left, n), side_terms(right, n)
    speed = jnp.maximum(tl[2], tr[2])
    fl, fr = side_flux(left, n, tl, speed), side_flux(right, n, tr, -speed)
    return [speed * (left[k] - right[k]) if k == 4 + n else fl[k] + fr[k] for k in range(8)]


def to_primitive(u):
    inv = 1.0 / u[0]
    v = [u[k] * inv for k in (1, 2, 3)]
    kin = u[1] * v[0] + u[2] * v[1] + u[3] * v[2]
    mag = u[4] * u[4] + u[5] * u[5] + u[6] * u[6]
    return [u[0], *v, u[4], u[5], u[6], (GAMMA - 1.0) * (u[7] - 0.5 * (kin + mag))]


def kernel(
    nx, ny, shift_ref, weight_ref, rho_in, vel_in, mag_in, pre_in, out_ref, rho_ref, vel_ref, mag_ref, pre_ref,
    u0, u1, w0, wh0, w1, wh1, ylo, yhi, sd0, sl0, sf0, sd1, sl1, sf1, pack, patch, xg, yg, out0, ring0, back0, got0, out1, ring1, back1, got1,
    xs, xr, ys, yr, ss, sr, ls,
):
    rows, nz, wide = rho_ref.shape
    half = nz // 2
    total_x = nx * rows
    total_y = ny * wide
    omega = 1.0 / (SHEAR_Q * total_x)
    share = 32 // ny
    prims, halves = (w0, w1), (wh0, wh1)
    carried = ((sd0, sl0, sf0), (sd1, sl1, sf1))
    spread = ((out0, ring0, back0, got0), (out1, ring1, back1, got1))
    gx = lax.axis_index("gx")
    gy = lax.axis_index("gy")
    first = gx == 0
    last = gx == nx - 1
    edge = jnp.logical_or(first, last)
    other = jnp.where(first, nx - 1, 0)
    north = lax.rem(gy + 1, ny)
    south = lax.rem(gy + ny - 1, ny)
    lane = lax.broadcasted_iota(jnp.int32, (2, half, wide), 2)
    quad = jnp.bitwise_and(lane, 3)
    even = jnp.bitwise_and(lane, 4) == 0
    inside = jnp.logical_and(lane >= 2, lane < wide - 2)

    loads = [
        pltpu.make_async_copy(src, dst, ls.at[k])
        for k, (src, dst) in enumerate(
            [(rho_in, rho_ref), (vel_in, vel_ref), (mag_in, mag_ref), (pre_in, pre_ref)]
        )
    ]
    for load in loads:
        load.start()

    barrier = pltpu.get_barrier_semaphore()

    def greet(x, y):
        pl.semaphore_signal(barrier, inc=1, device_id=(x, y), device_id_type=MESH)

    greet(gx, north)
    greet(gx, south)

    @pl.when(gx > 0)
    def _():
        greet(gx - 1, gy)

    @pl.when(gx < nx - 1)
    def _():
        greet(gx + 1, gy)

    def to_all(low, do):
        for step in range(low, ny):
            do(step)

    def each(low, high, do):
        def body(t, carry):
            do(t)
            return carry

        lax.fori_loop(low, high, body, 0)

    def peer(step):
        return jnp.bitwise_and(gy + step, ny - 1)

    @pl.when(edge)
    def _():
        to_all(1, lambda step: greet(gx, peer(step)))
        greet(other, gy)

    def await_greetings():
        pl.semaphore_wait(barrier, jnp.where(edge, 3 + ny, 4))

    def remote(src, dst, send, recv, x, y):
        return pltpu.make_async_remote_copy(
            src_ref=src, dst_ref=dst, send_sem=send, recv_sem=recv, device_id=(x, y), device_id_type=MESH
        )

    def radial(i):
        return (gx * rows + i).astype(jnp.float32) + (0.5 - 0.5 * total_x)

    def put_primitive(sec, i, prim):
        for k in range(8):
            prims[sec][k, i + 2] = prim[k]
            halves[sec][k, i + 2] = 0.5 * prim[k]

    def store_packs(sec):
        def some(t, carry):
            for k in [4 * t + j for j in range(4)]:
                both = []
                for odd in range(2):
                    acc = jnp.zeros((2, half, wide), jnp.float32)
                    slot = lax.shift_right_logical(jnp.bitwise_and(lane - 4 * odd, wide - 1), 3)
                    for i in range(odd, rows, 2):
                        moved = pltpu.roll(prims[sec][k, i + 2], (4 * i + 4) % wide, 2)
                        acc = jnp.where(slot == i // 2, moved, acc)
                    both.append(acc)
                pack[sec, 0, k] = pltpu.roll(jnp.where(even, both[1], both[0]), wide - 4, 2)
                pack[sec, 1, k] = jnp.where(even, both[0], both[1])
            return carry

        lax.fori_loop(0, 2, some, 0)

    def y_states(i, prim):
        for k in range(8):
            half_prim = 0.5 * prim[k]
            d = y_up(half_prim) - half_prim
            h = limited(d, y_down(d))
            ylo[k, i] = prim[k] + h
            yhi[k, i] = y_up(prim[k] - h)

    def start_row(i):
        def load(ref, *lead):
            return jnp.stack([ref[(*lead, i, pl.ds(z, half, stride=2), slice(None))] for z in range(2)])

        rho = load(rho_ref)
        v = [load(vel_ref, 0), load(vel_ref, 1) - SHEAR_Q * omega * radial(i), load(vel_ref, 2)]
        b = [load(mag_ref, k) for k in range(3)]
        p = load(pre_ref)
        m = [rho * v[k] for k in range(3)]
        kin = m[0] * v[0] + m[1] * v[1] + m[2] * v[2]
        mag = b[0] * b[0] + b[1] * b[1] + b[2] * b[2]
        energy = p * (1.0 / (GAMMA - 1.0)) + 0.5 * (kin + mag)
        for k, value in enumerate([rho, *m, *b, energy]):
            u0[k, i] = value
        prim = [rho, *v, *b, p]
        put_primitive(0, i, prim)
        y_states(i, prim)

    def merged(i, ref, k):
        back = pltpu.roll(patch[k], jnp.bitwise_and(wide - 2 - 4 * i, wide - 1), 2)
        return ref[k, i] + jnp.where(inside, 0.0, back)

    def middle_row(i):
        u = [merged(i, u1, k) for k in range(8)]
        for k in range(8):
            u1[k, i] = u[k]
        prim = to_primitive(u)
        put_primitive(1, i, prim)
        y_states(i, prim)

    def final_row(i):
        for k in range(8):
            value = merged(i, u0, k)
            for z in range(2):
                out_ref[k, i, pl.ds(z, half, stride=2), :] = value[z]

    def z_up(x):
        return jnp.stack([x[1], pltpu.roll(x[0], half - 1, 0)])

    def z_down(x):
        return jnp.stack([pltpu.roll(x[1], 1, 0), x[0]])

    def y_up(x):
        return pltpu.roll(x, wide - 1, 2)

    def y_down(x):
        return pltpu.roll(x, 1, 2)

    def z_change(whole, halved):
        left, right = [], []
        for k in range(8):
            d = z_up(halved[k]) - halved[k]
            h = limited(d, z_down(d))
            left.append(whole[k] + h)
            right.append(z_up(whole[k] - h))
        face = face_flux(left, right, 2)
        return [f - z_down(f) for f in face]

    def x_face(sec, i):
        w, wh = prims[sec], halves[sec]
        sd, sl, _ = carried[sec]
        left, right = [], []
        for k in range(8):
            d = wh[k, i + 4] - wh[k, i + 3]
            h = limited(d, sd[k])
            here = w[k, i + 3]
            left.append(sl[k])
            right.append(here - h)
            sd[k] = d
            sl[k] = here + h
        return face_flux(left, right, 0)

    def x_begin(sec, i):
        w, wh = prims[sec], halves[sec]
        sd, sl, sf = carried[sec]
        for k in range(8):
            before = wh[k, i + 1] - wh[k, i]
            d = wh[k, i + 2] - wh[k, i + 1]
            sd[k] = d
            sl[k] = w[k, i + 1] + limited(d, before)
        face = x_face(sec, i - 1)
        for k in range(8):
            sf[k] = face[k]

    def main_row(sec, i, carry):
        sf = carried[sec][2]
        whole = [prims[sec][k, i + 2] for k in range(8)]
        halved = [halves[sec][k, i + 2] for k in range(8)]
        dz = z_change(whole, halved)
        fy = face_flux([ylo[k, i] for k in range(8)], [yhi[k, i] for k in range(8)], 1)
        dy = [f - y_down(f) for f in fy]
        fx = x_face(sec, i)
        change = []
        for k in range(8):
            change.append((dz[k] + jnp.where(inside, dy[k], 0.0)) + (fx[k] - sf[k]))
            sf[k] = fx[k]
        ref = u1 if sec else u0
        u = [ref[k, i] for k in range(8)]
        step = 0.5 * TIME_STEP if sec else TIME_STEP
        r = radial(i)
        pull = (2.0 * SHEAR_Q * omega * omega * step) * r
        source = {
            1: (2.0 * omega * step) * u[2] + pull * u[0],
            2: (-2.0 * omega * step) * u[1],
            7: pull * u[1],
        }
        for k in range(8):
            base = 0.5 * (u0[k, i] + u[k]) if sec else u[k]
            value = base - (0.5 * step) * change[k]
            if k in source:
                value = value + source[k]
            (u0 if sec else u1)[k, i] = value
        return carry

    def edge_patch(sec):
        step = 0.5 * TIME_STEP if sec else TIME_STEP

        def turned(x, by):
            return x if by % wide == 0 else pltpu.roll(x, by % wide, 2)

        def rates(low, high, base):
            left, right = [], []
            for k in range(8):
                col = []
                for t in range(-1, 3):
                    start = t - base
                    take = quad < -start
                    if start >= 0:
                        col.append(turned(high[k], -start))
                    elif start == -4:
                        col.append(low[k])
                    elif start < -4:
                        col.append(turned(low[k], -4 - start))
                    else:
                        col.append(jnp.where(take, turned(low[k], -4 - start), turned(high[k], -start)))
                d = [0.5 * (col[t + 1] - col[t]) for t in range(3)]
                left.append(col[1] + limited(d[1], d[0]))
                right.append(col[2] - limited(d[2], d[1]))
            face = face_flux(left, right, 1)
            return [f - pltpu.roll(f, 1, 2) for f in face]

        low_side = rates([yg[sec, 0, k] for k in range(8)], [pack[sec, 0, k] for k in range(8)], 2)
        high_side = rates([pack[sec, 1, k] for k in range(8)], [yg[sec, 1, k] for k in range(8)], 4)
        for k in range(8):
            both = jnp.where(quad < 2, pltpu.roll(high_side[k], wide - 2, 2), low_side[k])
            patch[k] = (-0.5 * step) * both

    shift = shift_ref[0]
    weight = weight_ref[0].astype(jnp.float32) * WEIGHT_SCALE
    out_shift = jnp.where(first, total_y - 1 - shift, shift)
    out_weight = jnp.where(first, 1.0 - weight, weight)

    def gather_copy(sec, step):
        out, ring, _, _ = spread[sec]
        to = peer(step)
        return remote(out.at[to], ring.at[gy], ss.at[sec, 0], sr.at[sec, 0], gx, to)

    def hand_copy(sec, step):
        _, _, back, got = spread[sec]
        to = peer(step)
        return remote(back.at[to], got.at[gy], ss.at[sec, 1], sr.at[sec, 1], other, to)

    def all_gathered(sec):
        out, ring, _, _ = spread[sec]
        few = pl.ds(0, ny - 1)
        return remote(out.at[few], ring.at[few], ss.at[sec, 0], sr.at[sec, 0], gx, north)

    def all_handed(sec):
        _, _, back, got = spread[sec]
        return remote(back, got, ss.at[sec, 1], sr.at[sec, 1], other, gy)

    def parts(q):
        return q // 4, q // 2 % 2, q % 2

    def chain_start(sec, u):
        out, ring, _, _ = spread[sec]

        def fill(row):
            for q in range(32):
                k, j, z = parts(q)
                out[q // share, q % share] = u[k, row + j, z]

        pl.when(first)(lambda: fill(0))
        pl.when(last)(lambda: fill(rows - 2))

        @pl.when(edge)
        def _():
            ring[gy] = out[gy]

    def chain_send(sec):
        @pl.when(edge)
        def _():
            to_all(1, lambda step: gather_copy(sec, step).start())

    def chain_middle(sec):
        @pl.when(edge)
        def _():
            _, ring, back, _ = spread[sec]
            all_gathered(sec).wait_recv()
            blocks = lax.div(out_shift, wide)
            inner = lax.rem(out_shift, wide)
            src = lax.broadcasted_iota(jnp.int32, (wide, wide), 0)
            dst = lax.broadcasted_iota(jnp.int32, (wide, wide), 1)
            gap = dst - src - inner
            near = jnp.where(gap == 0, 1.0 - out_weight, 0.0) + jnp.where(gap == 1, out_weight, 0.0)
            far = jnp.where(gap == -wide, 1.0 - out_weight, 0.0) + jnp.where(gap == 1 - wide, out_weight, 0.0)

            def times(offset, m):
                x = jnp.stack([ring[lax.rem(j + 2 * ny - offset - blocks, ny)] for j in range(ny)])
                x = x.reshape(32 * half, wide)
                return jnp.dot(x, m, precision=lax.Precision.HIGHEST, preferred_element_type=jnp.float32)

            back[...] = (times(0, near) + times(1, far)).reshape(ny, share, half, wide)
            to_all(0, lambda step: hand_copy(sec, step).start())

    def chain_end(sec):
        @pl.when(edge)
        def _():
            got = spread[sec][3]
            all_handed(sec).wait_recv()
            delta = jnp.where(first, 1.0, -1.0)
            start = jnp.where(first, 0, rows + 2)
            for j in range(2):
                u = []
                for k in range(8):
                    at = [4 * k + 2 * j + z for z in range(2)]
                    u.append(jnp.stack([got[q // share, q % share] for q in at]))
                momentum = u[2] + u[0] * delta
                u[7] = u[7] + u[2] * delta + 0.5 * u[0]
                u[2] = momentum
                put_primitive(sec, start + j - 2, to_primitive(u))

    def x_copy(sec, side, incoming):
        away = gx - 1 if side == 0 else gx + 1
        w = prims[sec]
        own = w.at[:, 2:4] if side == 0 else w.at[:, rows : rows + 2]
        slot = side if incoming else 1 - side
        return remote(own, xg.at[sec, slot], xs.at[sec, side], xr.at[sec, slot], away, gy)

    def y_copy(sec, side, incoming):
        away = south if side == 0 else north
        slot = side if incoming else 1 - side
        return remote(pack.at[sec, side], yg.at[sec, slot], ys.at[sec, side], yr.at[sec, slot], gx, away)

    def on_side(side, do):
        pl.when(gx > 0 if side == 0 else gx < nx - 1)(do)

    def some_rows(sec, listed):
        for i in listed:
            (middle_row if sec else start_row)(i)

    def outer_rows(sec):
        some_rows(sec, (0, 1, rows - 2, rows - 1))

    def inner_rows(sec):
        each(0, rows // 4 - 1, lambda t: some_rows(sec, [4 * t + 2 + j for j in range(4)]))

    def send_rows(sec):
        for side in range(2):
            on_side(side, lambda: x_copy(sec, side, False).start())

    def send_columns(sec):
        for side in range(2):
            y_copy(sec, side, False).start()

    def take_columns(sec):
        for side in range(2):
            y_copy(sec, side, True).wait_recv()
        edge_patch(sec)

    early = jnp.where(last, 0, rows - 2)
    late = jnp.where(last, rows - 2, 0)

    def take_rows(sec):
        for side in range(2):

            def take():
                x_copy(sec, side, True).wait_recv()
                start = 0 if side == 0 else rows + 2
                for k in range(8):
                    value = xg[sec, side, k]
                    prims[sec][k, start : start + 2] = value
                    halves[sec][k, start : start + 2] = 0.5 * value

            on_side(side, take)

    def boundary_rows(sec, start):
        x_begin(sec, start)
        main(sec, start, start + 2)
        for j in range(2):
            (final_row if sec else middle_row)(start + j)

    def sent(sec):
        for side in range(2):
            on_side(side, lambda: x_copy(sec, side, False).wait_send())
            y_copy(sec, side, False).wait_send()

    def main(sec, low, high):
        lax.fori_loop(low, high, functools.partial(main_row, sec), 0)

    cuts = [min(max(c * rows // 32, 4), rows - 4) for c in CUTS]
    for load in loads:
        load.wait()
    outer_rows(0)
    chain_start(0, u0)
    inner_rows(0)
    await_greetings()
    chain_send(0)
    store_packs(0)
    x_begin(0, 2)
    main(0, 2, 8 * rows // 32)
    send_rows(0)
    send_columns(0)
    main(0, 8 * rows // 32, cuts[0])
    chain_middle(0)
    main(0, cuts[0], rows - 2)
    take_columns(0)
    inner_rows(1)
    x_begin(1, 4)
    main(1, 4, cuts[1])
    take_rows(0)
    boundary_rows(0, early)
    chain_end(0)
    boundary_rows(0, late)
    chain_start(1, u1)
    chain_send(1)
    store_packs(1)
    main(1, cuts[1], cuts[2] - 4 * rows // 32)
    send_rows(1)
    send_columns(1)
    main(1, cuts[2] - 4 * rows // 32, cuts[2])
    chain_middle(1)
    main(1, cuts[2], rows - 2)
    take_columns(1)
    x_begin(1, 2)
    main(1, 2, 4)
    each(1, rows // 2 - 1, lambda t: (final_row(2 * t), final_row(2 * t + 1)))
    take_rows(1)
    boundary_rows(1, early)
    chain_end(1)
    boundary_rows(1, late)
    sent(0)
    sent(1)

    @pl.when(edge)
    def _():
        for sec in range(2):
            all_gathered(sec).wait_send()
            all_handed(sec).wait_send()


def solution(mesh):
    nx, ny = mesh.shape["gx"], mesh.shape["gy"]

    def on_device(density, velocity, bfield, pressure, shear_shift, remap_weight):
        rows, nz, wide = density.shape
        half = nz // 2
        tile = (2, half, wide)
        slab = (8, 2, *tile)
        f32 = jnp.float32
        dma = pltpu.SemaphoreType.DMA
        vmem = pl.BlockSpec(memory_space=pltpu.VMEM)
        hbm = pl.BlockSpec(memory_space=pltpu.HBM)
        smem = pl.BlockSpec(memory_space=pltpu.SMEM)
        return pl.pallas_call(
            functools.partial(kernel, nx, ny),
            out_shape=jax.ShapeDtypeStruct((8, rows, nz, wide), f32),
            in_specs=[smem, smem, hbm, hbm, hbm, hbm],
            out_specs=vmem,
            scratch_shapes=[
                pltpu.VMEM((rows, nz, wide), f32),
                pltpu.VMEM((3, rows, nz, wide), f32),
                pltpu.VMEM((3, rows, nz, wide), f32),
                pltpu.VMEM((rows, nz, wide), f32),
                pltpu.VMEM((8, rows, *tile), f32),
                pltpu.VMEM((8, rows, *tile), f32),
                *[pltpu.VMEM((8, rows + 4, *tile), f32) for _ in range(4)],
                *[pltpu.VMEM((8, rows, *tile), f32) for _ in range(2)],
                *[pltpu.VMEM((8, *tile), f32) for _ in range(6)],
                pltpu.VMEM((2, 2, 8, *tile), f32),
                pltpu.VMEM((8, *tile), f32),
                pltpu.VMEM((2, 2, *slab), f32),
                pltpu.VMEM((2, 2, 8, *tile), f32),
                *[pltpu.VMEM((ny, 32 // ny, half, wide), f32) for _ in range(8)],
                dma((2, 2)),
                dma((2, 2)),
                dma((2, 2)),
                dma((2, 2)),
                dma((2, 2)),
                dma((2, 2)),
                dma((4,)),
            ],
            compiler_params=pltpu.CompilerParams(
                collective_id=0, has_side_effects=True, vmem_limit_bytes=40 * 1024 * 1024
            ),
        )(
            shear_shift.reshape(1),
            remap_weight.reshape(1),
            *[
                pltpu.with_memory_space_constraint(x, pltpu.HBM)
                for x in (density, velocity, bfield, pressure)
            ],
        )

    placed = (
        P("gx", None, "gy"),
        P(None, "gx", None, "gy"),
        P(None, "gx", None, "gy"),
        P("gx", None, "gy"),
        P(),
        P(),
    )
    return jax.shard_map(
        on_device, mesh=mesh, in_specs=placed, out_specs=P(None, "gx", None, "gy"), check_vma=False
    )
```
